32 devices in a mesh: dp: 8 (over z, y), mix: 4 (over x, core).
Axes of the slice: x: 2, y: 2, z: 4, core: 2. Of those that a mesh axis runs over, the one named last changes fastest.
Arguments:
- patches: bfloat16 [224, 196, 768], P('dp', 'mix'), may hold values from -6 to 6
- valid_counts: int32 [8], P('dp'), may hold values from 7 to 28, as said below
- gain_one: float32 [768], replicated, may hold values from 0.5 to 1.5
- shift_one: float32 [768], replicated, may hold values from -1.25 to 1.25
- tok_in: bfloat16 [196, 384], replicated, may hold values from -0.4375 to 0.4375
- tok_inbias: float32 [384], replicated, may hold values from -1.25 to 1.25
- tok_out: bfloat16 [384, 196], replicated, may hold values from -0.3125 to 0.3125
- tok_outbias: float32 [196], replicated, may hold values from -1.25 to 1.25
- gain_two: float32 [768], replicated, may hold values from 0.5 to 1.5
- shift_two: float32 [768], replicated, may hold values from -1.25 to 1.25
- chan_in: bfloat16 [768, 3072], replicated, may hold values from -0.21875 to 0.21875
- chan_inbias: float32 [3072], replicated, may hold values from -1.25 to 1.25
- chan_out: bfloat16 [3072, 768], replicated, may hold values from -0.109375 to 0.109375
- chan_outbias: float32 [768], replicated, may hold values from -1.25 to 1.25
- out_grad: bfloat16 [224, 196, 768], P('dp', 'mix'), may hold values from -6 to 6
Outputs:
- mixed_out: bfloat16 [224, 196, 768], P('dp', 'mix')
- patch_grad: bfloat16 [224, 196, 768], P('dp', 'mix')
- grad_gain_one: float32 [768], replicated
- grad_shift_one: float32 [768], replicated
- grad_tok_in: float32 [196, 384], replicated
- grad_tok_inbias: float32 [384], replicated
- grad_tok_out: float32 [384, 196], replicated
- grad_tok_outbias: float32 [196], replicated
- grad_gain_two: float32 [768], replicated
- grad_shift_two: float32 [768], replicated
- grad_chan_in: float32 [768, 3072], replicated
- grad_chan_inbias: float32 [3072], replicated
- grad_chan_out: float32 [3072, 768], replicated
- grad_chan_outbias: float32 [768], replicated
The draws below stay inside these ranges and needn't reach their ends.
Inputs may be any that keep to these rules, and one draw needn't show every extreme that they name: `valid_counts`: how many of the 28 images of each index of dp are real; the rest are padding and get no gradient.
All inputs are finite; a program needn't handle non-finite values.
Results may differ from the reference program's by a relative error of at most 0.008.
Values may be sent and summed in bfloat16 or wider, within the bound.
A program may use at most 192 MiB of HBM per device.

```python
import jax
import jax.numpy as jnp
from jax import lax

S = 196
DS = 384
D = 768
DC = 3072
IMG_DEV = 28
IMAGES = 224


def draw_valid_counts(key, part):
    groups = IMAGES // IMG_DEV
    least = max(IMG_DEV // 4, 1)
    first_key, second_key, third_key = jax.random.split(jax.random.fold_in(key, 7), 3)
    values = jax.random.randint(first_key, (groups,), least, IMG_DEV + 1)
    fullest = jax.random.randint(second_key, (), 0, groups)
    emptiest = (fullest + jax.random.randint(third_key, (), 1, groups)) % groups
    values = values.at[fullest].set(IMG_DEV).at[emptiest].set(least)
    return values.astype(jnp.int32)


def shard_levels(key, shape, shards, low, top_value):
    loudness = 1.0
    for axis_at, blocks in shards:
        heights = jax.random.uniform(jax.random.fold_in(jax.random.fold_in(key, 6), axis_at), (blocks,), jnp.float32, low / len(shards), top_value / len(shards))
        loudness = loudness * jnp.repeat(jnp.exp(heights), shape[axis_at] // blocks).reshape((-1,) + (1,) * (len(shape) - 1 - axis_at))
    return loudness


def noise(stream_key, shape, scale, most, shards=(), kind=jnp.bfloat16):
    level = shard_levels(stream_key, shape, shards, -0.22, 0.18) if shards else 1.0
    values = jax.random.normal(stream_key, shape, jnp.float32) * scale * level
    return jnp.minimum(jnp.maximum(values, -most), most).astype(kind)


def setup_inputs(seed: int = 0) -> dict:
    splits = jax.random.split(jax.random.key(seed), 16)
    return {
        "patches": noise(splits[0], (IMAGES, S, D), 1.0, 6.0, ((0, 8), (1, 4))),
        "valid_counts": draw_valid_counts(jax.random.fold_in(splits[15], 71), 0),
        "gain_one": jnp.clip(1.0 + 0.1 * jax.random.normal(splits[2], (D,), jnp.float32), 0.5, 1.5),
        "shift_one": noise(splits[3], (D,), 0.2, 1.25, (), jnp.float32),
        "tok_in": noise(splits[4], (S, DS), S ** -0.5, 0.4375),
        "tok_inbias": noise(splits[5], (DS,), 0.2, 1.25, (), jnp.float32),
        "tok_out": noise(splits[6], (DS, S), DS ** -0.5, 0.3125),
        "tok_outbias": noise(splits[7], (S,), 0.2, 1.25, (), jnp.float32),
        "gain_two": jnp.clip(1.0 + 0.1 * jax.random.normal(splits[8], (D,), jnp.float32), 0.5, 1.5),
        "shift_two": noise(splits[9], (D,), 0.2, 1.25, (), jnp.float32),
        "chan_in": noise(splits[10], (D, DC), D ** -0.5, 0.21875),
        "chan_inbias": noise(splits[11], (DC,), 0.2, 1.25, (), jnp.float32),
        "chan_out": noise(splits[12], (DC, D), DC ** -0.5, 0.109375),
        "chan_outbias": noise(splits[13], (D,), 0.2, 1.25, (), jnp.float32),
        "out_grad": noise(splits[14], (IMAGES, S, D), 1.0, 6.0, ((0, 8), (1, 4))),
    }


EPS = 1e-06

@jax.custom_vjp
def low(v):
    return lax.optimization_barrier(v.astype(jnp.bfloat16)).astype(jnp.float32)

@jax.custom_vjp
def low_back(v):
    return v

def low_keep(v):
    return (low(v), None)

def low_pass(kept, grad):
    return (grad,)

def back_keep(v):
    return (v, None)

def back_low(kept, grad):
    return (low(grad),)
low.defvjp(low_keep, low_pass)
low_back.defvjp(back_keep, back_low)

def layer_norm(values, gain, shift):
    center = values - lax.optimization_barrier(jnp.mean(values, axis=-1, keepdims=True))
    spread = lax.optimization_barrier(jnp.mean(center * center, axis=-1, keepdims=True))
    return center * lax.rsqrt(spread + EPS) * gain + shift

def block(inputs, params):
    gain_one, shift_one, tok_in, tok_inbias, tok_out, tok_outbias, gain_two, shift_two, chan_in, chan_inbias, chan_out, chan_outbias = params
    highest = lax.Precision.HIGHEST
    normed = low_back(low(layer_norm(inputs, gain_one, shift_one)))
    widened = low_back(jnp.einsum('bsc,sk->bkc', normed, tok_in, precision=highest) + tok_inbias[None, :, None])
    hidden = low(jax.nn.gelu(widened))
    mixed = low_back(low(jnp.einsum('bkc,ks->bsc', hidden, tok_out, precision=highest) + tok_outbias[None, :, None]))
    middle = inputs + mixed
    second = low(layer_norm(middle, gain_two, shift_two))
    inner = low_back(jnp.einsum('bsc,cf->bsf', second, chan_in, precision=highest) + chan_inbias)
    activ = low(jax.nn.gelu(inner))
    return middle + jnp.einsum('bsf,fc->bsc', activ, chan_out, precision=highest) + chan_outbias

def reference(patches, valid_counts, gain_one, shift_one, tok_in, tok_inbias, tok_out, tok_outbias, gain_two, shift_two, chan_in, chan_inbias, chan_out, chan_outbias, out_grad):
    params = tuple((p.astype(jnp.float32) for p in (gain_one, shift_one, tok_in, tok_inbias, tok_out, tok_outbias, gain_two, shift_two, chan_in, chan_inbias, chan_out, chan_outbias)))
    inputs = patches.astype(jnp.float32).reshape(-1, IMG_DEV, S, D)
    cotangents = out_grad.astype(jnp.float32).reshape(-1, IMG_DEV, S, D)
    places = jnp.arange(IMG_DEV, dtype=jnp.int32)
    masks = (places[None, :] < valid_counts.astype(jnp.int32)[:, None]).astype(jnp.float32)

    def step(total, items):
        group_in, group_grad, group_mask = items
        result, backward = jax.vjp(block, group_in, params)
        input_grad, param_grads = backward(group_grad * group_mask[:, None, None])
        total = jax.tree.map(jnp.add, total, param_grads)
        return (total, (result.astype(jnp.bfloat16), input_grad.astype(jnp.bfloat16)))
    zeros = jax.tree.map(jnp.zeros_like, params)
    total, (outputs, input_grads) = lax.scan(step, zeros, (inputs, cotangents, masks))
    return (outputs.reshape(IMAGES, S, D), input_grads.reshape(IMAGES, S, D), total[0], total[1], total[2], total[3], total[4], total[5], total[6], total[7], total[8], total[9], total[10], total[11])
```

```python
import functools

import jax
import jax.numpy as jnp
from jax import lax
from jax.experimental import pallas as pl
from jax.experimental.pallas import tpu as pltpu
from jax.sharding import PartitionSpec as P

EPS = 1e-06
SQ = 0.7978845608028654
CU = 0.044715
GROUP = 8
SLAB = 64
FC = 256
NT = (((1,), (1,)), ((), ()))
F32 = jnp.float32
BF16 = jnp.bfloat16
MESH = pl.DeviceIdType.MESH


def gelu_and_slope(v):
    v2 = v * v
    t = jnp.tanh(v * (SQ + (SQ * CU) * v2))
    h = 0.5 * v
    return h + h * t, 0.5 + 0.5 * t + h * (1.0 - t * t) * (SQ + (3.0 * SQ * CU) * v2)


def gelu(v):
    h = 0.5 * v
    return h + h * jnp.tanh(v * (SQ + (SQ * CU) * (v * v)))


def normalise(v):
    c = v - jnp.mean(v, axis=-1, keepdims=True)
    r = lax.rsqrt(jnp.mean(c * c, axis=-1, keepdims=True) + EPS)
    return c * r, r


def dot(a, b):
    return jnp.dot(a, b, preferred_element_type=F32)


def dot_nt(a, b):
    return lax.dot_general(a, b, NT, preferred_element_type=F32)


def flip(index, bit, step):
    return index + step - 2 * step * bit


def layer_kernel(
    dims,
    patches,
    out_grad,
    valid,
    tok_in,
    tok_out_t,
    chan_in,
    chan_out,
    gain_one,
    shift_one,
    gain_two,
    shift_two,
    tok_inbias,
    tok_outbias,
    chan_inbias,
    chan_outbias,
    mixed_out,
    patch_grad,
    sums,
    w1,
    w2,
    xin,
    uin,
    mo,
    rows32,
    tin,
    tin_t,
    tout,
    tout_t,
    mixed_keep,
    sec,
    sec_t,
    ups,
    ups_t,
    gsec,
    gi_s,
    act_s,
    d_tin,
    d_tout,
    vecs,
    d_b1,
    d_tb,
    blk,
    r0,
    r1,
    r2,
    r3,
    r4,
    wsem,
    osem,
    xs_s,
    xs_r,
    us_s,
    us_r,
    ms_s,
    ms_r,
    ps_s,
    ps_r,
    as_s,
    as_r,
    free,
):
    ni, part, width, ds, dc = dims
    nc = dc // FC
    rows = 4 * SLAB
    last = nc + ni
    me = lax.axis_index("mix")
    dp = lax.axis_index("dp")
    core = lax.rem(me, 2)
    xb = me // 2
    yb = lax.rem(dp, 2)
    zab = lax.rem(dp // 2, 2)
    zbb = lax.rem(dp // 4, 2)
    sib = flip(me, core, 1)
    xp = flip(me, xb, 2)
    diag = 3 - me
    peers = (xp, diag, sib)
    dev_sib = (dp, sib)
    dev_x = (dp, xp)
    dev_y = (flip(dp, yb, 1), me)
    dev_za = (flip(dp, zab, 2), me)
    dev_zb = (flip(dp, zbb, 4), me)

    wcopy1 = pltpu.make_async_copy(chan_in, w1, wsem.at[0])
    wcopy2 = pltpu.make_async_copy(chan_out, w2, wsem.at[1])
    wcopy1.start()
    wcopy2.start()

    barrier = pltpu.get_barrier_semaphore()
    for dev in ((dp, xp), (dp, diag), dev_sib, dev_y, dev_za, dev_zb):
        pl.semaphore_signal(barrier, inc=1, device_id=dev, device_id_type=MESH)
    pl.semaphore_wait(barrier, 6)

    def gather_copy(src, dst, ssem, rsem, i, q):
        return pltpu.make_async_remote_copy(
            src_ref=src.at[q * ni + i],
            dst_ref=dst.at[i, me],
            send_sem=ssem.at[i, q],
            recv_sem=rsem.at[i, me],
            device_id=(dp, q),
            device_id_type=MESH,
        )

    def gather_from(src, dst, ssem, rsem, i, q):
        return pltpu.make_async_remote_copy(
            src_ref=src.at[q * ni + i],
            dst_ref=dst.at[i, q],
            send_sem=ssem.at[i, q],
            recv_sem=rsem.at[i, q],
            device_id=(dp, q),
            device_id_type=MESH,
        )

    def gather_own(src, dst, rsem, i):
        return pltpu.make_async_copy(src.at[me * ni + i], dst.at[i, me], rsem.at[i, me])

    def return_copy(src, dst, ssem, rsem, i, q):
        return pltpu.make_async_remote_copy(
            src_ref=src.at[i, q],
            dst_ref=dst.at[me * ni + i],
            send_sem=ssem.at[i, q],
            recv_sem=rsem.at[i, me],
            device_id=(dp, q),
            device_id_type=MESH,
        )

    def return_from(src, dst, ssem, rsem, i, q):
        return pltpu.make_async_remote_copy(
            src_ref=src.at[i, q],
            dst_ref=dst.at[q * ni + i],
            send_sem=ssem.at[i, q],
            recv_sem=rsem.at[i, q],
            device_id=(dp, q),
            device_id_type=MESH,
        )

    def return_own(src, dst, ssem, i):
        return pltpu.make_async_copy(src.at[i, me], dst.at[me * ni + i], ssem.at[i, me])

    def each_image(fn):
        def body(i, carry):
            fn(i)
            return carry

        lax.fori_loop(0, ni, body, 0)

    def send_patches(i):
        for q in peers:
            gather_copy(patches, xin, xs_s, xs_r, i, q).start()
        gather_own(patches, xin, xs_r, i).start()

    each_image(send_patches)

    rows32[...] = jnp.zeros_like(rows32)
    for w_in, w_row, w_col in ((tok_in, tin, tin_t), (tok_out_t, tout_t, tout)):
        wide = w_in[...].astype(F32)
        rows32[:, :ds] = jnp.zeros((rows, ds), F32)
        for s in range(4):
            rows32[s * SLAB : s * SLAB + part, :ds] = wide[s * part : (s + 1) * part]
        full = rows32[:, :ds]
        w_row[...] = full.astype(BF16)
        w_col[...] = full.T.astype(BF16)
    rows32[...] = jnp.zeros_like(rows32)
    d_tin[...] = jnp.zeros_like(d_tin)
    d_tout[...] = jnp.zeros_like(d_tout)
    vecs[...] = jnp.zeros_like(vecs)
    d_tb[...] = jnp.zeros_like(d_tb)

    def widen_rows(ref, i):
        for s in range(4):
            rows32[s * SLAB : s * SLAB + part, :] = ref[i, s].astype(F32)
        return rows32[...]

    def image_rows(i):
        return pl.ds(pl.multiple_of(i * rows, rows), rows)

    wcopy1.wait()
    wcopy2.wait()

    def forward(i):
        for q in peers:
            gather_from(patches, xin, xs_s, xs_r, i, q).wait_recv()
        gather_own(patches, xin, xs_r, i).wait()
        for q in peers:
            gather_copy(out_grad, uin, us_s, us_r, i, q).start()
        gather_own(out_grad, uin, us_r, i).start()
        at = image_rows(i)
        x = widen_rows(xin, i)
        xh, _ = normalise(x)
        normed = (xh * gain_one[...] + shift_one[...]).astype(BF16)
        hidden = gelu(dot(tin_t[...], normed) + tok_inbias[...]).astype(BF16)
        mixed = (dot(tout_t[...], hidden) + tok_outbias[...]).astype(BF16)
        mixed_keep[at, :] = mixed
        middle = x + mixed.astype(F32)
        xh, _ = normalise(middle)
        second = xh * gain_two[...] + shift_two[...]
        sec[at, :] = second.astype(BF16)
        sec_t[:, at] = second.T.astype(BF16)
        gsec[at, :] = middle + chan_outbias[...]

        def hidden_block(c, carry):
            cs = pl.ds(pl.multiple_of(c * 768, 768), 768)
            activ = gelu(dot(sec[at, :], w1[:, cs]) + chan_inbias[:, cs]).astype(BF16)
            gsec[at, :] += dot(activ, w2[cs, :])
            return carry

        lax.fori_loop(0, dc // 768, hidden_block, 0)
        for s in range(4):
            base = pl.multiple_of(i * rows, rows) + s * SLAB
            mo[i, s] = gsec[pl.ds(base, SLAB), :][:part].astype(BF16)

    each_image(forward)

    def take_upstream(i):
        for q in peers:
            gather_from(out_grad, uin, us_s, us_r, i, q).wait_recv()
        gather_own(out_grad, uin, us_r, i).wait()
        for q in peers:
            return_copy(mo, mixed_out, ms_s, ms_r, i, q).start()
        return_own(mo, mixed_out, ms_s, i).start()
        at = image_rows(i)
        up = widen_rows(uin, i)
        up = jnp.where(me * ni + i < valid[0], up, 0.0)
        ups[at, :] = up.astype(BF16)
        ups_t[:, at] = up.T.astype(BF16)
        vecs[4:5, :] += jnp.sum(up, axis=0, keepdims=True)

    each_image(take_upstream)

    gsec[...] = jnp.zeros_like(gsec)

    def chunk_compute(c):
        cs = pl.ds(pl.multiple_of(c * FC, FC), FC)
        activ, slope = gelu_and_slope(dot(sec[...], w1[:, cs]) + chan_inbias[:, cs])
        act_s[...] = activ.astype(BF16)
        gi = (dot_nt(ups[...], w2[cs, :]) * slope).astype(BF16)
        gi_s[...] = gi
        d_b1[:, cs] = jnp.sum(gi.astype(F32), axis=0, keepdims=True)
        gsec[...] += dot_nt(gi_s[...], w1[:, cs])
        blk[c, 0] = dot(sec_t[...], gi_s[...]).astype(BF16)
        blk[c, 1] = dot(ups_t[...], act_s[...]).astype(BF16)

    def image_backward(i):
        for q in peers:
            return_copy(mo, mixed_out, ms_s, ms_r, i, q).wait_send()
        return_own(mo, mixed_out, ms_s, i).wait()
        at = image_rows(i)
        x = widen_rows(xin, i)
        xh, r = normalise(x + mixed_keep[at, :].astype(F32))
        gs = gsec[at, :]
        vecs[2:3, :] += jnp.sum(gs * xh, axis=0, keepdims=True)
        vecs[3:4, :] += jnp.sum(gs, axis=0, keepdims=True)
        q = gs * gain_two[...]
        gm = ups[at, :].astype(F32) + r * (
            q - jnp.mean(q, axis=-1, keepdims=True) - xh * jnp.mean(q * xh, axis=-1, keepdims=True)
        )
        gmb = gm.astype(BF16)
        xh, r = normalise(x)
        normed = (xh * gain_one[...] + shift_one[...]).astype(BF16)
        hid, slope = gelu_and_slope(dot(tin_t[...], normed) + tok_inbias[...])
        gw = (dot(tout[...], gmb) * slope).astype(BF16)
        d_tout[...] += dot_nt(gmb, hid.astype(BF16))
        d_tin[...] += dot_nt(normed, gw)
        ones = jnp.ones((8, width), BF16)
        d_tb[:, :ds] += dot_nt(ones, gw)
        d_tb[:, ds : ds + rows] += dot_nt(ones, gmb)
        gn = dot(tin[...], gw).astype(BF16).astype(F32)
        vecs[0:1, :] += jnp.sum(gn * xh, axis=0, keepdims=True)
        vecs[1:2, :] += jnp.sum(gn, axis=0, keepdims=True)
        q = gn * gain_one[...]
        pg = gm + r * (
            q - jnp.mean(q, axis=-1, keepdims=True) - xh * jnp.mean(q * xh, axis=-1, keepdims=True)
        )
        for s in range(4):
            mo[i, s] = pg[s * SLAB : s * SLAB + part].astype(BF16)
        for p in peers:
            return_copy(mo, patch_grad, ps_s, ps_r, i, p).start()
        return_own(mo, patch_grad, ps_s, i).start()

    def pack_small():
        for j in range(ds // 128):
            cols = slice(j * 128, (j + 1) * 128)
            blk[nc, 0, j * rows : (j + 1) * rows, :128] = d_tin[:, cols].astype(BF16)
            blk[nc, 1, j * rows : (j + 1) * rows, :128] = d_tout[:, cols].astype(BF16)
        blk[nc, 0, :, 128:] = jnp.zeros((width, 128), BF16)
        blk[nc, 1, :, 128:] = jnp.zeros((width, 128), BF16)
        at = 0
        for v, n in (
            [(vecs[k : k + 1, :], width) for k in range(5)]
            + [(d_tb[0:1, :], ds + rows)]
            + [(d_b1[...], dc)]
        ):
            for j in range(n // 128):
                rows32[at : at + 1, :128] = v[:, j * 128 : (j + 1) * 128]
                at += 1
        up = -(-at // 16) * 16
        blk[nc, 0, :up, 128:] = rows32[:up, :128].astype(BF16)

    def stage_device(k, c):
        swap = lax.rem(c, 4) // 3
        dev1 = (dev_y[0] + swap * (dp - dev_y[0]), me + swap * (xp - me))
        dev4 = (dp + swap * (dev_y[0] - dp), xp + swap * (me - xp))
        return (dev_sib, dev1, dev_za, dev_zb, dev4, dev_zb, dev_za, dev1, dev_sib)[k]

    def stage(k, c, cc):
        swap = lax.rem(c, 4) // 3
        b1 = yb + swap * (xb - yb)
        half, quarter, eighth = width // 2, width // 4, width // 8
        o1 = b1 * half
        n1 = (1 - b1) * half
        o2 = o1 + zab * quarter
        n2 = o1 + (1 - zab) * quarter
        o3 = o2 + zbb * eighth
        n3 = o2 + (1 - zbb) * eighth
        own = blk.at[cc, core]

        def piece(start, size):
            return own.at[pl.ds(pl.multiple_of(start, 16), size), :]

        kept = (own, piece(o1, half), piece(o2, quarter), piece(o3, eighth), piece(o3, eighth))
        src = (
            blk.at[cc, 1 - core],
            piece(n1, half),
            piece(n2, quarter),
            piece(n3, eighth),
            piece(o3, eighth),
            piece(o3, eighth),
            piece(o2, quarter),
            piece(o1, half),
            own,
        )[k]
        land = (r0.at[lax.rem(cc, 4)], r1.at[cc], r2.at[cc], r3.at[cc], r4.at[cc])
        copy = pltpu.make_async_remote_copy(
            src_ref=src,
            dst_ref=land[k] if k < 5 else src,
            send_sem=as_s.at[k, cc],
            recv_sem=as_r.at[k, cc],
            device_id=stage_device(k, c),
            device_id_type=MESH,
        )
        return copy, (kept[k] if k < 5 else None), (land[k] if k < 5 else None)

    def export(cc):
        return pltpu.make_async_copy(blk.at[cc], sums.at[cc], osem.at[cc])

    def tick(t, carry):
        for k in reversed(range(9)):
            c = t - 1 - k

            @pl.when(jnp.logical_and(c >= 0, jnp.logical_or(c < nc, c == last)))
            def _(k=k, c=c):
                cc = jnp.minimum(c, nc)
                copy, kept, land = stage(k, c, cc)
                copy.wait()
                if k < 4:
                    dev = stage_device(k, c)
                    pl.semaphore_signal(free.at[k, cc], inc=1, device_id=dev, device_id_type=MESH)
                if kept is not None:
                    kept[...] = (kept[...].astype(F32) + land[...].astype(F32)).astype(BF16)
                if k < 8:
                    if k >= 4:
                        pl.semaphore_wait(free.at[7 - k, cc], 1)
                    stage(k + 1, c, cc)[0].start()
                else:
                    export(cc).start()

        @pl.when(t < nc)
        def _():
            chunk_compute(t)

        @pl.when(jnp.logical_and(t >= nc, t < last))
        def _():
            image_backward(t - nc)

        @pl.when(t == last)
        def _():
            pack_small()

        @pl.when(jnp.logical_or(t < nc, t == last))
        def _():
            stage(0, t, jnp.minimum(t, nc))[0].start()

        return carry

    lax.fori_loop(0, last + 10, tick, 0)

    def finish(i):
        for q in peers:
            gather_copy(patches, xin, xs_s, xs_r, i, q).wait_send()
            gather_copy(out_grad, uin, us_s, us_r, i, q).wait_send()
            return_from(mo, mixed_out, ms_s, ms_r, i, q).wait_recv()
            return_copy(mo, patch_grad, ps_s, ps_r, i, q).wait_send()
            return_from(mo, patch_grad, ps_s, ps_r, i, q).wait_recv()
        return_own(mo, patch_grad, ps_s, i).wait()

    each_image(finish)

    def exported(c, carry):
        export(c).wait()
        return carry

    lax.fori_loop(0, nc + 1, exported, 0)


def spread_kernel(dims, block, small, chan_in, chan_out, tok_in, tok_out_t, vecs, tok_b, b1):
    ni, part, width, ds, dc = dims
    rows = 4 * SLAB
    chan_in[...] = block[0, 0].astype(F32)
    chan_out[...] = block[0, 1].astype(F32).T

    @pl.when(pl.program_id(0) == 0)
    def _():
        for m, ref in ((0, tok_in), (1, tok_out_t)):
            for j in range(ds // 128):
                v = small[0, m, j * rows : (j + 1) * rows, :128].astype(F32)
                for s in range(4):
                    ref[s * part : (s + 1) * part, j * 128 : (j + 1) * 128] = v[
                        s * SLAB : s * SLAB + part
                    ]
        v = small[0, 0, :rows, 128:].astype(F32)
        at = 0
        for k in range(5):
            for j in range(width // 128):
                vecs[k : k + 1, j * 128 : (j + 1) * 128] = v[at : at + 1]
                at += 1
        for j in range((ds + rows) // 128):
            tok_b[:, j * 128 : (j + 1) * 128] = v[at : at + 1]
            at += 1
        for j in range(dc // 128):
            b1[:, j * 128 : (j + 1) * 128] = v[at : at + 1]
            at += 1


def slab_rows(vector, part):
    return jnp.pad(vector.reshape(4, part), ((0, 0), (0, SLAB - part))).reshape(4 * SLAB, 1)


def shards(
    mesh_shape,
    patches,
    valid_counts,
    gain_one,
    shift_one,
    tok_in,
    tok_inbias,
    tok_out,
    tok_outbias,
    gain_two,
    shift_two,
    chan_in,
    chan_inbias,
    chan_out,
    chan_outbias,
    out_grad,
):
    images, part, width = patches.shape
    s_all, ds = tok_in.shape
    dc = chan_in.shape[1]
    ni = images // 4
    rows = 4 * SLAB
    total = ni * rows
    nc = dc // FC
    dims = (ni, part, width, ds, dc)
    anywhere = pl.BlockSpec(memory_space=pl.ANY)
    vmem = pl.BlockSpec(memory_space=pltpu.VMEM)
    dma = pltpu.SemaphoreType.DMA
    row = lambda v: v.reshape(1, -1)
    mixed_out, patch_grad, sums = pl.pallas_call(
        functools.partial(layer_kernel, dims),
        name="layer",
        out_shape=(
            jax.ShapeDtypeStruct(patches.shape, BF16),
            jax.ShapeDtypeStruct(patches.shape, BF16),
            jax.ShapeDtypeStruct((nc + 1, 2, width, FC), BF16),
        ),
        in_specs=[anywhere] * 2
        + [pl.BlockSpec(memory_space=pltpu.SMEM)]
        + [vmem] * 2
        + [anywhere] * 2
        + [vmem] * 8,
        out_specs=(anywhere,) * 3,
        scratch_shapes=[
            pltpu.VMEM((width, dc), BF16),
            pltpu.VMEM((dc, width), BF16),
            pltpu.VMEM((ni, 4, part, width), BF16),
            pltpu.VMEM((ni, 4, part, width), BF16),
            pltpu.VMEM((ni, 4, part, width), BF16),
            pltpu.VMEM((rows, width), F32),
            pltpu.VMEM((rows, ds), BF16),
            pltpu.VMEM((ds, rows), BF16),
            pltpu.VMEM((ds, rows), BF16),
            pltpu.VMEM((rows, ds), BF16),
            pltpu.VMEM((total, width), BF16),
            pltpu.VMEM((total, width), BF16),
            pltpu.VMEM((width, total), BF16),
            pltpu.VMEM((total, width), BF16),
            pltpu.VMEM((width, total), BF16),
            pltpu.VMEM((total, width), F32),
            pltpu.VMEM((total, FC), BF16),
            pltpu.VMEM((total, FC), BF16),
            pltpu.VMEM((rows, ds), F32),
            pltpu.VMEM((rows, ds), F32),
            pltpu.VMEM((8, width), F32),
            pltpu.VMEM((1, dc), F32),
            pltpu.VMEM((8, ds + rows), F32),
            pltpu.VMEM((nc + 1, 2, width, FC), BF16),
            pltpu.VMEM((4, width, FC), BF16),
            pltpu.VMEM((nc + 1, width // 2, FC), BF16),
            pltpu.VMEM((nc + 1, width // 4, FC), BF16),
            pltpu.VMEM((nc + 1, width // 8, FC), BF16),
            pltpu.VMEM((nc + 1, width // 8, FC), BF16),
            dma((2,)),
            dma((nc + 1,)),
        ]
        + [dma((ni, 4))] * 8
        + [dma((9, nc + 1))] * 2
        + [pltpu.SemaphoreType.REGULAR((4, nc + 1))],
        compiler_params=pltpu.CompilerParams(
            collective_id=0, has_side_effects=True, vmem_limit_bytes=63 << 20
        ),
        cost_estimate=pl.CostEstimate(
            flops=14 * total * width * dc,
            bytes_accessed=40 << 20,
            transcendentals=total * dc,
        ),
    )(
        patches,
        out_grad,
        valid_counts,
        tok_in,
        tok_out.T,
        chan_in,
        chan_out,
        row(gain_one),
        row(shift_one),
        row(gain_two),
        row(shift_two),
        tok_inbias.reshape(ds, 1),
        slab_rows(tok_outbias, part),
        row(chan_inbias),
        row(chan_outbias),
    )
    g_chan_in, g_chan_out, g_tok_in, g_tok_out_t, vecs, tok_b, b1 = pl.pallas_call(
        functools.partial(spread_kernel, dims),
        name="spread",
        grid=(nc,),
        out_shape=(
            jax.ShapeDtypeStruct((width, dc), F32),
            jax.ShapeDtypeStruct((dc, width), F32),
            jax.ShapeDtypeStruct((s_all, ds), F32),
            jax.ShapeDtypeStruct((s_all, ds), F32),
            jax.ShapeDtypeStruct((5, width), F32),
            jax.ShapeDtypeStruct((1, ds + rows), F32),
            jax.ShapeDtypeStruct((1, dc), F32),
        ),
        in_specs=[
            pl.BlockSpec((1, 2, width, FC), lambda c: (c, 0, 0, 0)),
            pl.BlockSpec((1, 2, width, FC), lambda c: (nc, 0, 0, 0)),
        ],
        out_specs=(
            pl.BlockSpec((width, FC), lambda c: (0, c)),
            pl.BlockSpec((FC, width), lambda c: (c, 0)),
            pl.BlockSpec((s_all, ds), lambda c: (0, 0)),
            pl.BlockSpec((s_all, ds), lambda c: (0, 0)),
            pl.BlockSpec((5, width), lambda c: (0, 0)),
            pl.BlockSpec((1, ds + rows), lambda c: (0, 0)),
            pl.BlockSpec((1, dc), lambda c: (0, 0)),
        ),
        compiler_params=pltpu.CompilerParams(vmem_limit_bytes=32 << 20),
    )(sums, sums)
    grads = (
        vecs[0],
        vecs[1],
        g_tok_in,
        tok_b[0, :ds],
        g_tok_out_t.T,
        tok_b[0, ds:].reshape(4, SLAB)[:, :part].reshape(s_all),
        vecs[2],
        vecs[3],
        g_chan_in,
        b1[0],
        g_chan_out,
        vecs[4],
    )
    if mesh_shape["dp"] > GROUP:
        count = mesh_shape["dp"] // GROUP
        groups = [[g * GROUP + j for g in range(count)] for j in range(GROUP)]
        grads = lax.psum(grads, "dp", axis_index_groups=groups)
    return (mixed_out, patch_grad) + grads


def solution(mesh):
    whole, split = P(), P("dp", "mix", None)
    return jax.shard_map(
        functools.partial(shards, dict(mesh.shape)),
        mesh=mesh,
        in_specs=(split, P("dp")) + (whole,) * 12 + (split,),
        out_specs=(split, split) + (whole,) * 12,
        check_vma=False,
    )
```

```python
import functools

import jax
import jax.numpy as jnp
from jax import lax
from jax.experimental import pallas as pl
from jax.experimental.pallas import tpu as pltpu
from jax.sharding import PartitionSpec as P

EPS = 1e-06
SQ = 0.7978845608028654
CU = 0.044715
GROUP = 8
WAIT = (2, 4, 6, 7, 8, 9, 11, 13, 14)
SLAB = 64
FC = 256
NT = (((1,), (1,)), ((), ()))
F32 = jnp.float32
BF16 = jnp.bfloat16
MESH = pl.DeviceIdType.MESH


def gelu_and_slope(v):
    v2 = v * v
    t = jnp.tanh(v * (SQ + (SQ * CU) * v2))
    h = 0.5 * v
    return h + h * t, 0.5 + 0.5 * t + h * (1.0 - t * t) * (SQ + (3.0 * SQ * CU) * v2)


def gelu(v):
    h = 0.5 * v
    return h + h * jnp.tanh(v * (SQ + (SQ * CU) * (v * v)))


def normalise(v):
    c = v - jnp.mean(v, axis=-1, keepdims=True)
    r = lax.rsqrt(jnp.mean(c * c, axis=-1, keepdims=True) + EPS)
    return c * r, r


def dot(a, b):
    return jnp.dot(a, b, preferred_element_type=F32)


def dot_nt(a, b):
    return lax.dot_general(a, b, NT, preferred_element_type=F32)


def flip(index, bit, step):
    return index + step - 2 * step * bit


def layer_kernel(
    dims,
    patches,
    out_grad,
    valid,
    tok_in,
    tok_out_t,
    chan_in,
    chan_out,
    gain_one_flat,
    shift_one_flat,
    gain_two_flat,
    shift_two_flat,
    tok_inbias_flat,
    tok_outbias_flat,
    chan_inbias,
    chan_outbias_flat,
    mixed_out,
    patch_grad,
    sums,
    w1,
    w2,
    xin,
    uin,
    mo,
    rows32,
    tin,
    tin_t,
    tout,
    tout_t,
    mixed_keep,
    sec,
    sec_t,
    ups,
    ups_t,
    gsec,
    gi_s,
    act_s,
    d_tin,
    d_tout,
    vecs,
    d_b1,
    d_tb,
    gain_one,
    shift_one,
    gain_two,
    shift_two,
    chan_outbias,
    tok_inbias,
    tok_outbias,
    blk,
    r0,
    r1,
    r2,
    r3,
    r4,
    wsem,
    osem,
    xs_s,
    xs_r,
    us_s,
    us_r,
    ms_s,
    ms_r,
    ps_s,
    ps_r,
    as_s,
    as_r,
    free,
):
    ni, part, width, ds, dc = dims
    nc = dc // FC
    rows = 4 * SLAB
    me = lax.axis_index("mix")
    dp = lax.axis_index("dp")
    core = lax.rem(me, 2)
    xb = me // 2
    yb = lax.rem(dp, 2)
    zab = lax.rem(dp // 2, 2)
    zbb = lax.rem(dp // 4, 2)
    sib = flip(me, core, 1)
    xp = flip(me, xb, 2)
    diag = 3 - me
    peers = (xp, diag, sib)
    dev_sib = (dp, sib)
    dev_x = (dp, xp)
    dev_y = (flip(dp, yb, 1), me)
    dev_za = (flip(dp, zab, 2), me)
    dev_zb = (flip(dp, zbb, 4), me)

    wcopy1 = pltpu.make_async_copy(chan_in, w1, wsem.at[0])
    wcopy2 = pltpu.make_async_copy(chan_out, w2, wsem.at[1])
    wcopy1.start()
    wcopy2.start()

    barrier = pltpu.get_barrier_semaphore()
    for dev in ((dp, xp), (dp, diag), dev_sib, dev_y, dev_za, dev_zb):
        pl.semaphore_signal(barrier, inc=1, device_id=dev, device_id_type=MESH)
    pl.semaphore_wait(barrier, 6)

    def gather_copy(src, dst, ssem, rsem, i, q):
        return pltpu.make_async_remote_copy(
            src_ref=src.at[q * ni + i],
            dst_ref=dst.at[i, me],
            send_sem=ssem.at[i, q],
            recv_sem=rsem.at[i, me],
            device_id=(dp, q),
            device_id_type=MESH,
        )

    def gather_from(src, dst, ssem, rsem, i, q):
        return pltpu.make_async_remote_copy(
            src_ref=src.at[q * ni + i],
            dst_ref=dst.at[i, q],
            send_sem=ssem.at[i, q],
            recv_sem=rsem.at[i, q],
            device_id=(dp, q),
            device_id_type=MESH,
        )

    def gather_own(src, dst, rsem, i):
        return pltpu.make_async_copy(src.at[me * ni + i], dst.at[i, me], rsem.at[i, me])

    def return_copy(src, dst, ssem, rsem, i, q):
        return pltpu.make_async_remote_copy(
            src_ref=src.at[i, q],
            dst_ref=dst.at[me * ni + i],
            send_sem=ssem.at[i, q],
            recv_sem=rsem.at[i, me],
            device_id=(dp, q),
            device_id_type=MESH,
        )

    def return_from(src, dst, ssem, rsem, i, q):
        return pltpu.make_async_remote_copy(
            src_ref=src.at[i, q],
            dst_ref=dst.at[q * ni + i],
            send_sem=ssem.at[i, q],
            recv_sem=rsem.at[i, q],
            device_id=(dp, q),
            device_id_type=MESH,
        )

    def return_own(src, dst, ssem, i):
        return pltpu.make_async_copy(src.at[i, me], dst.at[me * ni + i], ssem.at[i, me])

    def each_image(fn):
        def body(i, carry):
            fn(i)
            return carry

        lax.fori_loop(0, ni, body, 0)

    def send_patches(i):
        for q in peers:
            gather_copy(patches, xin, xs_s, xs_r, i, q).start()
        gather_own(patches, xin, xs_r, i).start()

    each_image(send_patches)

    rows32[...] = jnp.zeros_like(rows32)
    for w_in, w_row, w_col in ((tok_in, tin, tin_t), (tok_out_t, tout_t, tout)):
        wide = w_in[...].astype(F32)
        rows32[:, :ds] = jnp.zeros((rows, ds), F32)
        for s in range(4):
            rows32[s * SLAB : s * SLAB + part, :ds] = wide[s * part : (s + 1) * part]
        full = rows32[:, :ds]
        w_row[...] = full.astype(BF16)
        w_col[...] = full.T.astype(BF16)
    for flat, row in (
        (gain_one_flat, gain_one),
        (shift_one_flat, shift_one),
        (gain_two_flat, gain_two),
        (shift_two_flat, shift_two),
        (chan_outbias_flat, chan_outbias),
    ):
        row[...] = flat[...].reshape(1, width)
    tok_inbias[...] = jnp.broadcast_to(tok_inbias_flat[...].reshape(1, ds), (8, ds)).T[:, :1]
    rows32[...] = jnp.zeros_like(rows32)
    rows32[:1, : 4 * part] = tok_outbias_flat[...].reshape(1, 4 * part)
    column = rows32[:8, :rows].T
    rows32[...] = jnp.zeros_like(rows32)
    for s in range(4):
        rows32[s * SLAB : s * SLAB + part, :8] = column[s * part : (s + 1) * part]
    tok_outbias[...] = rows32[:, :1]
    rows32[...] = jnp.zeros_like(rows32)
    d_tin[...] = jnp.zeros_like(d_tin)
    d_tout[...] = jnp.zeros_like(d_tout)
    vecs[...] = jnp.zeros_like(vecs)
    d_tb[...] = jnp.zeros_like(d_tb)

    def widen_rows(ref, i):
        for s in range(4):
            rows32[s * SLAB : s * SLAB + part, :] = ref[i, s].astype(F32)
        return rows32[...]

    def image_rows(i):
        return pl.ds(pl.multiple_of(i * rows, rows), rows)

    wcopy1.wait()
    wcopy2.wait()

    def forward(i):
        for q in peers:
            gather_from(patches, xin, xs_s, xs_r, i, q).wait_recv()
        gather_own(patches, xin, xs_r, i).wait()
        for q in peers:
            gather_copy(out_grad, uin, us_s, us_r, i, q).start()
        gather_own(out_grad, uin, us_r, i).start()
        at = image_rows(i)
        x = widen_rows(xin, i)
        xh, _ = normalise(x)
        normed = (xh * gain_one[...] + shift_one[...]).astype(BF16)
        hidden = gelu(dot(tin_t[...], normed) + tok_inbias[...]).astype(BF16)
        mixed = (dot(tout_t[...], hidden) + tok_outbias[...]).astype(BF16)
        mixed_keep[at, :] = mixed
        middle = x + mixed.astype(F32)
        xh, _ = normalise(middle)
        second = xh * gain_two[...] + shift_two[...]
        sec[at, :] = second.astype(BF16)
        sec_t[:, at] = second.T.astype(BF16)
        gsec[at, :] = middle + chan_outbias[...]

        def hidden_block(c, carry):
            cs = pl.ds(pl.multiple_of(c * 768, 768), 768)
            activ = gelu(dot(sec[at, :], w1[:, cs]) + chan_inbias[:, cs]).astype(BF16)
            gsec[at, :] += dot(activ, w2[cs, :])
            return carry

        lax.fori_loop(0, dc // 768, hidden_block, 0, unroll=True)
        for s in range(4):
            base = pl.multiple_of(i * rows, rows) + s * SLAB
            mo[i, s] = gsec[pl.ds(base, SLAB), :][:part].astype(BF16)

    def take_upstream(i):
        for q in peers:
            gather_from(out_grad, uin, us_s, us_r, i, q).wait_recv()
        gather_own(out_grad, uin, us_r, i).wait()
        at = image_rows(i)
        up = widen_rows(uin, i)
        up = jnp.where(me * ni + i < valid[0], up, 0.0)
        ups[at, :] = up.astype(BF16)
        ups_t[:, at] = up.T.astype(BF16)
        vecs[4:5, :] += jnp.sum(up, axis=0, keepdims=True)

    late = min(3, ni)

    def arrive(i):
        @pl.when(i < ni)
        def _():
            forward(i)

        @pl.when(i >= late)
        def _():
            take_upstream(i - late)

    def arrive_step(i, carry):
        arrive(i)
        return carry

    lax.fori_loop(0, ni + late, arrive_step, 0)

    def send_mixed(i):
        for q in peers:
            return_copy(mo, mixed_out, ms_s, ms_r, i, q).start()
        return_own(mo, mixed_out, ms_s, i).start()

    gsec[...] = jnp.zeros_like(gsec)

    def chunk_compute(c):
        cs = pl.ds(pl.multiple_of(c * FC, FC), FC)
        activ, slope = gelu_and_slope(dot(sec[...], w1[:, cs]) + chan_inbias[:, cs])
        act_s[...] = activ.astype(BF16)
        gi = (dot_nt(ups[...], w2[cs, :]) * slope).astype(BF16)
        gi_s[...] = gi
        d_b1[:, cs] = jnp.sum(gi.astype(F32), axis=0, keepdims=True)
        gsec[...] += dot_nt(gi_s[...], w1[:, cs])
        blk[c, 0] = dot(sec_t[...], gi_s[...]).astype(BF16)
        blk[c, 1] = dot(ups_t[...], act_s[...]).astype(BF16)

    def image_backward(i):
        for q in peers:
            return_copy(mo, mixed_out, ms_s, ms_r, i, q).wait_send()
        return_own(mo, mixed_out, ms_s, i).wait()
        at = image_rows(i)
        x = widen_rows(xin, i)
        xh, r = normalise(x + mixed_keep[at, :].astype(F32))
        gs = gsec[at, :]
        vecs[2:3, :] += jnp.sum(gs * xh, axis=0, keepdims=True)
        vecs[3:4, :] += jnp.sum(gs, axis=0, keepdims=True)
        q = gs * gain_two[...]
        gm = ups[at, :].astype(F32) + r * (
            q - jnp.mean(q, axis=-1, keepdims=True) - xh * jnp.mean(q * xh, axis=-1, keepdims=True)
        )
        gmb = gm.astype(BF16)
        xh, r = normalise(x)
        normed = (xh * gain_one[...] + shift_one[...]).astype(BF16)
        hid, slope = gelu_and_slope(dot(tin_t[...], normed) + tok_inbias[...])
        gw = (dot(tout[...], gmb) * slope).astype(BF16)
        d_tout[...] += dot_nt(gmb, hid.astype(BF16))
        d_tin[...] += dot_nt(normed, gw)
        ones = jnp.ones((8, width), BF16)
        d_tb[:, :ds] += dot_nt(ones, gw)
        d_tb[:, ds : ds + rows] += dot_nt(ones, gmb)
        gn = dot(tin[...], gw).astype(BF16).astype(F32)
        vecs[0:1, :] += jnp.sum(gn * xh, axis=0, keepdims=True)
        vecs[1:2, :] += jnp.sum(gn, axis=0, keepdims=True)
        q = gn * gain_one[...]
        pg = gm + r * (
            q - jnp.mean(q, axis=-1, keepdims=True) - xh * jnp.mean(q * xh, axis=-1, keepdims=True)
        )
        for s in range(4):
            mo[i, s] = pg[s * SLAB : s * SLAB + part].astype(BF16)
        for p in peers:
            return_copy(mo, patch_grad, ps_s, ps_r, i, p).start()
        return_own(mo, patch_grad, ps_s, i).start()

    def pack_small():
        for j in range(ds // 128):
            cols = slice(j * 128, (j + 1) * 128)
            blk[nc, 0, j * rows : (j + 1) * rows, :128] = d_tin[:, cols].astype(BF16)
            blk[nc, 1, j * rows : (j + 1) * rows, :128] = d_tout[:, cols].astype(BF16)
        blk[nc, 0, :, 128:] = jnp.zeros((width, 128), BF16)
        blk[nc, 1, :, 128:] = jnp.zeros((width, 128), BF16)
        at = 0
        for v, n in (
            [(vecs[k : k + 1, :], width) for k in range(5)]
            + [(d_tb[0:1, :], ds + rows)]
            + [(d_b1[...], dc)]
        ):
            for j in range(n // 128):
                rows32[at : at + 1, :128] = v[:, j * 128 : (j + 1) * 128]
                at += 1
        up = -(-at // 16) * 16
        blk[nc, 0, :up, 128:] = rows32[:up, :128].astype(BF16)

    def stage_device(k, c):
        swap = lax.rem(c, 4) // 3
        dev1 = (dev_y[0] + swap * (dp - dev_y[0]), me + swap * (xp - me))
        dev4 = (dp + swap * (dev_y[0] - dp), xp + swap * (me - xp))
        return (dev_sib, dev1, dev_za, dev_zb, dev4, dev_zb, dev_za, dev1, dev_sib)[k]

    def stage(k, c):
        swap = lax.rem(c, 4) // 3
        b1 = yb + swap * (xb - yb)
        half, quarter, eighth = width // 2, width // 4, width // 8
        o1 = b1 * half
        n1 = (1 - b1) * half
        o2 = o1 + zab * quarter
        n2 = o1 + (1 - zab) * quarter
        o3 = o2 + zbb * eighth
        n3 = o2 + (1 - zbb) * eighth
        own = blk.at[c, core]

        def piece(start, size):
            return own.at[pl.ds(pl.multiple_of(start, 16), size), :]

        kept = (own, piece(o1, half), piece(o2, quarter), piece(o3, eighth), piece(o3, eighth))
        src = (
            blk.at[c, 1 - core],
            piece(n1, half),
            piece(n2, quarter),
            piece(n3, eighth),
            piece(o3, eighth),
            piece(o3, eighth),
            piece(o2, quarter),
            piece(o1, half),
            own,
        )[k]
        land = (r0.at[lax.rem(c, 4)], r1.at[c], r2.at[c], r3.at[c], r4.at[c])
        copy = pltpu.make_async_remote_copy(
            src_ref=src,
            dst_ref=land[k] if k < 5 else src,
            send_sem=as_s.at[k, c],
            recv_sem=as_r.at[k, c],
            device_id=stage_device(k, c),
            device_id_type=MESH,
        )
        return copy, (kept[k] if k < 5 else None), (land[k] if k < 5 else None)

    def export(c):
        return pltpu.make_async_copy(blk.at[c], sums.at[c], osem.at[c])

    def step(u, carry):
        for k in reversed(range(9)):
            c = u - WAIT[k]

            @pl.when(jnp.logical_and(c >= 0, c <= nc))
            def _(k=k, c=c):
                copy, kept, land = stage(k, c)
                copy.wait()
                if k < 4:
                    dev = stage_device(k, c)
                    pl.semaphore_signal(free.at[k, c], inc=1, device_id=dev, device_id_type=MESH)
                if kept is not None:
                    kept[...] = (kept[...].astype(F32) + land[...].astype(F32)).astype(BF16)
                if k < 8:
                    if k >= 4:
                        pl.semaphore_wait(free.at[7 - k, c], 1)
                    stage(k + 1, c)[0].start()
                else:
                    export(c).start()

        @pl.when(u < ni)
        def _():
            send_mixed(u)

        @pl.when(u <= nc)
        def _():
            def quantum(w, carry):
                @pl.when(w < nc)
                def _():
                    chunk_compute(w)

                @pl.when(w >= nc)
                def _():
                    image_backward(w - nc)

                return carry

            lead = nc // 2

            def done(n):
                rest = jnp.maximum(n - lead, 0) * (nc + ni - lead) // (nc + 1 - lead)
                return jnp.minimum(n, lead) + rest

            lax.fori_loop(done(u), done(u + 1), quantum, 0)

            @pl.when(u == nc)
            def _():
                pack_small()

            stage(0, u)[0].start()

        return carry

    lax.fori_loop(0, nc + 1 + WAIT[-1], step, 0)

    def finish(i):
        for q in peers:
            gather_copy(patches, xin, xs_s, xs_r, i, q).wait_send()
            gather_copy(out_grad, uin, us_s, us_r, i, q).wait_send()
            return_from(mo, mixed_out, ms_s, ms_r, i, q).wait_recv()
            return_copy(mo, patch_grad, ps_s, ps_r, i, q).wait_send()
            return_from(mo, patch_grad, ps_s, ps_r, i, q).wait_recv()
        return_own(mo, patch_grad, ps_s, i).wait()

    each_image(finish)

    def exported(c, carry):
        export(c).wait()
        return carry

    lax.fori_loop(0, nc + 1, exported, 0)


def spread_kernel(
    dims,
    block,
    small,
    mixed_from,
    patch_from,
    chan_in,
    chan_out,
    tok_in,
    tok_out_t,
    gain_one,
    shift_one,
    tok_inbias,
    tok_outbias,
    gain_two,
    shift_two,
    chan_inbias,
    chan_outbias,
    mixed_to,
    patch_to,
    hold,
    sem,
):
    ni, part, width, ds, dc = dims
    rows = 4 * SLAB
    loads = (
        pltpu.make_async_copy(mixed_from, hold.at[0], sem.at[0]),
        pltpu.make_async_copy(patch_from, hold.at[1], sem.at[1]),
    )
    stores = (
        pltpu.make_async_copy(hold.at[0], mixed_to, sem.at[2]),
        pltpu.make_async_copy(hold.at[1], patch_to, sem.at[3]),
    )

    @pl.when(pl.program_id(0) == 0)
    def _():
        for copy in loads:
            copy.start()

    @pl.when(pl.program_id(0) == 3)
    def _():
        for load, store in zip(loads, stores):
            load.wait()
            store.start()

    @pl.when(pl.program_id(0) == pl.num_programs(0) - 1)
    def _():
        for store in stores:
            store.wait()

    chan_in[...] = block[0, 0].astype(F32)
    chan_out[...] = block[0, 1].astype(F32).T

    @pl.when(pl.program_id(0) == 0)
    def _():
        for m, ref in ((0, tok_in), (1, tok_out_t)):
            for j in range(ds // 128):
                v = small[0, m, j * rows : (j + 1) * rows, :128].astype(F32)
                for s in range(4):
                    ref[s * part : (s + 1) * part, j * 128 : (j + 1) * 128] = v[
                        s * SLAB : s * SLAB + part
                    ]
        v = small[0, 0, :rows, 128:].astype(F32)
        at = 0
        for ref, n in (
            (gain_one, width),
            (shift_one, width),
            (gain_two, width),
            (shift_two, width),
            (chan_outbias, width),
            (tok_inbias, ds),
            (tok_outbias, rows),
            (chan_inbias, dc),
        ):
            flat = jnp.concatenate([v[at + j : at + j + 1] for j in range(n // 128)], axis=1)
            at += n // 128
            if ref is tok_outbias:
                flat = jnp.concatenate(
                    [flat[:, s * SLAB : s * SLAB + part] for s in range(4)], axis=1
                )
            ref[...] = flat.reshape(ref.shape)


def shards(
    mesh_shape,
    patches,
    valid_counts,
    gain_one,
    shift_one,
    tok_in,
    tok_inbias,
    tok_out,
    tok_outbias,
    gain_two,
    shift_two,
    chan_in,
    chan_inbias,
    chan_out,
    chan_outbias,
    out_grad,
):
    images, part, width = patches.shape
    s_all, ds = tok_in.shape
    dc = chan_in.shape[1]
    ni = images // 4
    rows = 4 * SLAB
    total = ni * rows
    nc = dc // FC
    dims = (ni, part, width, ds, dc)
    anywhere = pl.BlockSpec(memory_space=pl.ANY)
    vmem = pl.BlockSpec(memory_space=pltpu.VMEM)
    dma = pltpu.SemaphoreType.DMA
    mixed_here, patch_here, sums = pl.pallas_call(
        functools.partial(layer_kernel, dims),
        name="layer",
        out_shape=(
            jax.ShapeDtypeStruct(patches.shape, BF16),
            jax.ShapeDtypeStruct(patches.shape, BF16),
            jax.ShapeDtypeStruct((nc + 1, 2, width, FC), BF16),
        ),
        in_specs=[anywhere] * 2
        + [pl.BlockSpec(memory_space=pltpu.SMEM)]
        + [vmem] * 2
        + [anywhere] * 2
        + [vmem] * 8,
        out_specs=(anywhere,) * 3,
        scratch_shapes=[
            pltpu.VMEM((width, dc), BF16),
            pltpu.VMEM((dc, width), BF16),
            pltpu.VMEM((ni, 4, part, width), BF16),
            pltpu.VMEM((ni, 4, part, width), BF16),
            pltpu.VMEM((ni, 4, part, width), BF16),
            pltpu.VMEM((rows, width), F32),
            pltpu.VMEM((rows, ds), BF16),
            pltpu.VMEM((ds, rows), BF16),
            pltpu.VMEM((ds, rows), BF16),
            pltpu.VMEM((rows, ds), BF16),
            pltpu.VMEM((total, width), BF16),
            pltpu.VMEM((total, width), BF16),
            pltpu.VMEM((width, total), BF16),
            pltpu.VMEM((total, width), BF16),
            pltpu.VMEM((width, total), BF16),
            pltpu.VMEM((total, width), F32),
            pltpu.VMEM((total, FC), BF16),
            pltpu.VMEM((total, FC), BF16),
            pltpu.VMEM((rows, ds), F32),
            pltpu.VMEM((rows, ds), F32),
            pltpu.VMEM((8, width), F32),
            pltpu.VMEM((1, dc), F32),
            pltpu.VMEM((8, ds + rows), F32),
            pltpu.VMEM((1, width), F32),
            pltpu.VMEM((1, width), F32),
            pltpu.VMEM((1, width), F32),
            pltpu.VMEM((1, width), F32),
            pltpu.VMEM((1, width), F32),
            pltpu.VMEM((ds, 1), F32),
            pltpu.VMEM((rows, 1), F32),
            pltpu.VMEM((nc + 1, 2, width, FC), BF16),
            pltpu.VMEM((4, width, FC), BF16),
            pltpu.VMEM((nc + 1, width // 2, FC), BF16),
            pltpu.VMEM((nc + 1, width // 4, FC), BF16),
            pltpu.VMEM((nc + 1, width // 8, FC), BF16),
            pltpu.VMEM((nc + 1, width // 8, FC), BF16),
            dma((2,)),
            dma((nc + 1,)),
        ]
        + [dma((ni, 4))] * 8
        + [dma((9, nc + 1))] * 2
        + [pltpu.SemaphoreType.REGULAR((4, nc + 1))],
        compiler_params=pltpu.CompilerParams(
            collective_id=0, has_side_effects=True, vmem_limit_bytes=63 << 20
        ),
        cost_estimate=pl.CostEstimate(
            flops=14 * total * width * dc,
            bytes_accessed=40 << 20,
            transcendentals=total * dc,
        ),
    )(
        patches,
        out_grad,
        valid_counts,
        tok_in,
        tok_out.T,
        chan_in,
        chan_out,
        gain_one,
        shift_one,
        gain_two,
        shift_two,
        tok_inbias,
        tok_outbias,
        chan_inbias.reshape(1, dc),
        chan_outbias,
    )
    vec = lambda n: (jax.ShapeDtypeStruct((n,), F32), pl.BlockSpec((n,), lambda c: (0,)))
    vectors = [vec(n) for n in (width, width, ds, s_all, width, width, dc, width)]
    out = pl.pallas_call(
        functools.partial(spread_kernel, dims),
        name="spread",
        grid=(nc,),
        out_shape=(
            jax.ShapeDtypeStruct((width, dc), F32),
            jax.ShapeDtypeStruct((dc, width), F32),
            jax.ShapeDtypeStruct((s_all, ds), F32),
            jax.ShapeDtypeStruct((s_all, ds), F32),
        )
        + tuple(v[0] for v in vectors)
        + (
            jax.ShapeDtypeStruct(patches.shape, BF16),
            jax.ShapeDtypeStruct(patches.shape, BF16),
        ),
        in_specs=[
            pl.BlockSpec((1, 2, width, FC), lambda c: (c, 0, 0, 0)),
            pl.BlockSpec((1, 2, width, FC), lambda c: (nc, 0, 0, 0)),
            anywhere,
            anywhere,
        ],
        out_specs=(
            pl.BlockSpec((width, FC), lambda c: (0, c)),
            pl.BlockSpec((FC, width), lambda c: (c, 0)),
            pl.BlockSpec((s_all, ds), lambda c: (0, 0)),
            pl.BlockSpec((s_all, ds), lambda c: (0, 0)),
        )
        + tuple(v[1] for v in vectors)
        + (anywhere, anywhere),
        scratch_shapes=[pltpu.VMEM((2,) + patches.shape, BF16), dma((4,))],
        compiler_params=pltpu.CompilerParams(vmem_limit_bytes=63 << 20),
    )(sums, sums, mixed_here, patch_here)
    g_chan_in, g_chan_out, g_tok_in, g_tok_out_t = out[:4]
    g_one, s_one, b_tin, b_tout, g_two, s_two, b_cin, b_cout, mixed_out, patch_grad = out[4:]
    grads = (
        g_one,
        s_one,
        g_tok_in,
        b_tin,
        g_tok_out_t.T,
        b_tout,
        g_two,
        s_two,
        g_chan_in,
        b_cin,
        g_chan_out,
        b_cout,
    )
    if mesh_shape["dp"] > GROUP:
        count = mesh_shape["dp"] // GROUP
        groups = [[g * GROUP + j for g in range(count)] for j in range(GROUP)]
        grads = lax.psum(grads, "dp", axis_index_groups=groups)
    return (mixed_out, patch_grad) + grads


def solution(mesh):
    whole, split = P(), P("dp", "mix", None)
    return jax.shard_map(
        functools.partial(shards, dict(mesh.shape)),
        mesh=mesh,
        in_specs=(split, P("dp")) + (whole,) * 12 + (split,),
        out_specs=(split, split) + (whole,) * 12,
        check_vma=False,
    )
```

```python
import functools

import jax
import jax.numpy as jnp
from jax import lax
from jax.experimental import pallas as pl
from jax.experimental.pallas import tpu as pltpu
from jax.sharding import PartitionSpec as P

EPS = 1e-06
SQ = 0.7978845608028654
CU = 0.044715
GROUP = 8
WIDE = 2
LEAD = 8
EXTRA = 4
WAIT = (2, 4, 6, 8, 10, 12, 14, 17, 19)
SLAB = 64
FC = 256
SPLIT = 512
NT = (((1,), (1,)), ((), ()))
F32 = jnp.float32
BF16 = jnp.bfloat16
MESH = pl.DeviceIdType.MESH


def gelu_and_slope(v):
    v2 = v * v
    p = 0.5 + 0.5 * jnp.tanh(v * (SQ + (SQ * CU) * v2))
    g = v * p
    return g, p + g * (1.0 - p) * (2.0 * SQ + (6.0 * SQ * CU) * v2)


def gelu(v):
    return v * (0.5 + 0.5 * jnp.tanh(v * (SQ + (SQ * CU) * (v * v))))


def normalise(v):
    c = v - jnp.mean(v, axis=-1, keepdims=True)
    r = lax.rsqrt(jnp.mean(c * c, axis=-1, keepdims=True) + EPS)
    return c * r, r


def dot(a, b):
    return jnp.dot(a, b, preferred_element_type=F32)


def dot_nt(a, b):
    return lax.dot_general(a, b, NT, preferred_element_type=F32)


def spare_row(n, part):
    spare = SLAB - part
    return n // spare * SLAB + part + n % spare


def flip(index, bit, step):
    return index + step - 2 * step * bit


def layer_kernel(
    dims,
    patches,
    out_grad,
    valid,
    tok_in,
    tok_out_t,
    chan_in,
    chan_out,
    gain_one_flat,
    shift_one_flat,
    gain_two_flat,
    shift_two_flat,
    tok_inbias_flat,
    tok_outbias_flat,
    chan_inbias,
    chan_outbias_flat,
    mixed_out,
    patch_grad,
    sums,
    w1,
    w2,
    xin,
    uin,
    mo,
    rows32,
    tin,
    tin_t,
    tout,
    tout_t,
    mixed_keep,
    sec,
    sec_t,
    ups,
    ups_t,
    gsec,
    gi_s,
    act_s,
    d_tin,
    d_tout,
    vecs,
    d_b1,
    d_tb,
    gain_one,
    shift_one,
    gain_two,
    shift_two,
    chan_outbias,
    tok_inbias,
    tok_outbias,
    blk,
    r0,
    r1,
    r2,
    r3,
    r4,
    wsem,
    osem,
    xs_s,
    xs_r,
    us_s,
    us_r,
    ms_s,
    ms_r,
    ps_s,
    ps_r,
    as_s,
    as_r,
    free,
):
    ni, part, width, ds, dc = dims
    nc = dc // FC
    rows = 4 * SLAB
    me = lax.axis_index("mix")
    dp = lax.axis_index("dp")
    core = lax.rem(me, 2)
    xb = me // 2
    yb = lax.rem(dp, 2)
    zab = lax.rem(dp // 2, 2)
    zbb = lax.rem(dp // 4, 2)
    sib = flip(me, core, 1)
    xp = flip(me, xb, 2)
    diag = 3 - me
    peers = (xp, diag, sib)
    dev_sib = (dp, sib)
    dev_x = (dp, xp)
    dev_y = (flip(dp, yb, 1), me)
    dev_za = (flip(dp, zab, 2), me)
    dev_zb = (flip(dp, zbb, 4), me)

    wcopy1 = pltpu.make_async_copy(chan_in, w1, wsem.at[0])
    wcopy2 = pltpu.make_async_copy(chan_out, w2, wsem.at[1])
    wcopy1.start()
    wcopy2.start()

    barrier = pltpu.get_barrier_semaphore()
    for dev in ((dp, xp), (dp, diag), dev_sib, dev_y, dev_za, dev_zb):
        pl.semaphore_signal(barrier, inc=1, device_id=dev, device_id_type=MESH)
    pl.semaphore_wait(barrier, 6)

    def gather_copy(src, dst, ssem, rsem, i, q):
        return pltpu.make_async_remote_copy(
            src_ref=src.at[q * ni + i],
            dst_ref=dst.at[i, me],
            send_sem=ssem.at[i, q],
            recv_sem=rsem.at[i, me],
            device_id=(dp, q),
            device_id_type=MESH,
        )

    def gather_from(src, dst, ssem, rsem, i, q):
        return pltpu.make_async_remote_copy(
            src_ref=src.at[q * ni + i],
            dst_ref=dst.at[i, q],
            send_sem=ssem.at[i, q],
            recv_sem=rsem.at[i, q],
            device_id=(dp, q),
            device_id_type=MESH,
        )

    def gather_own(src, dst, rsem, i):
        return pltpu.make_async_copy(src.at[me * ni + i], dst.at[i, me], rsem.at[i, me])

    def return_copy(src, dst, ssem, rsem, i, q):
        return pltpu.make_async_remote_copy(
            src_ref=src.at[i, q],
            dst_ref=dst.at[me * ni + i],
            send_sem=ssem.at[i, q],
            recv_sem=rsem.at[i, me],
            device_id=(dp, q),
            device_id_type=MESH,
        )

    def return_from(src, dst, ssem, rsem, i, q):
        return pltpu.make_async_remote_copy(
            src_ref=src.at[i, q],
            dst_ref=dst.at[q * ni + i],
            send_sem=ssem.at[i, q],
            recv_sem=rsem.at[i, q],
            device_id=(dp, q),
            device_id_type=MESH,
        )

    def return_own(src, dst, ssem, i):
        return pltpu.make_async_copy(src.at[i, me], dst.at[me * ni + i], ssem.at[i, me])

    def each_image(fn):
        def body(i, carry):
            fn(i)
            return carry

        lax.fori_loop(0, ni, body, 0)

    def send_patches(i):
        for q in peers:
            gather_copy(patches, xin, xs_s, xs_r, i, q).start()
        gather_own(patches, xin, xs_r, i).start()

    each_image(send_patches)

    rows32[...] = jnp.zeros_like(rows32)
    for w_in, w_row, w_col in ((tok_in, tin, tin_t), (tok_out_t, tout_t, tout)):
        wide = w_in[...].astype(F32)
        rows32[:, :ds] = jnp.zeros((rows, ds), F32)
        for s in range(4):
            rows32[s * SLAB : s * SLAB + part, :ds] = wide[s * part : (s + 1) * part]
        full = rows32[:, :ds]
        w_row[...] = full.astype(BF16)
        w_col[...] = full.T.astype(BF16)
    for flat, row in (
        (gain_one_flat, gain_one),
        (shift_one_flat, shift_one),
        (gain_two_flat, gain_two),
        (shift_two_flat, shift_two),
        (chan_outbias_flat, chan_outbias),
    ):
        row[...] = flat[...].reshape(1, width)
    tok_inbias[...] = jnp.broadcast_to(tok_inbias_flat[...].reshape(1, ds), (8, ds)).T[:, :1]
    rows32[...] = jnp.zeros_like(rows32)
    rows32[:1, : 4 * part] = tok_outbias_flat[...].reshape(1, 4 * part)
    column = rows32[:8, :rows].T
    rows32[...] = jnp.zeros_like(rows32)
    for s in range(4):
        rows32[s * SLAB : s * SLAB + part, :8] = column[s * part : (s + 1) * part]
    tok_outbias[...] = rows32[:, :1]
    rows32[...] = jnp.zeros_like(rows32)
    d_tin[...] = jnp.zeros_like(d_tin)
    d_tout[...] = jnp.zeros_like(d_tout)
    vecs[...] = jnp.zeros_like(vecs)
    d_tb[...] = jnp.zeros_like(d_tb)

    def widen_rows(ref, i):
        for s in range(4):
            rows32[s * SLAB : s * SLAB + part, :] = ref[i, s].astype(F32)
        return rows32[...]

    def image_rows(i):
        return pl.ds(pl.multiple_of(i * rows, rows), rows)

    wcopy1.wait()
    wcopy2.wait()

    def forward(i):
        for q in peers:
            gather_from(patches, xin, xs_s, xs_r, i, q).wait_recv()
        gather_own(patches, xin, xs_r, i).wait()
        for q in peers:
            gather_copy(out_grad, uin, us_s, us_r, i, q).start()
        gather_own(out_grad, uin, us_r, i).start()
        at = image_rows(i)
        x = widen_rows(xin, i)
        xh, _ = normalise(x)
        normed = (xh * gain_one[...] + shift_one[...]).astype(BF16)
        hidden = gelu(dot(tin_t[...], normed) + tok_inbias[...]).astype(BF16)
        mixed = (dot(tout_t[...], hidden) + tok_outbias[...]).astype(BF16)
        mixed_keep[at, :] = mixed
        middle = x + mixed.astype(F32)
        xh, _ = normalise(middle)
        second = xh * gain_two[...] + shift_two[...]
        sec[at, :] = second.astype(BF16)
        sec_t[:, at] = second.T.astype(BF16)
        gsec[at, :] = middle + chan_outbias[...]

        def hidden_block(c, carry):
            cs = pl.ds(pl.multiple_of(c * 768, 768), 768)
            activ = gelu(dot(sec[at, :], w1[:, cs]) + chan_inbias[:, cs]).astype(BF16)
            gsec[at, :] += dot(activ, w2[cs, :])
            return carry

        lax.fori_loop(0, dc // 768, hidden_block, 0, unroll=True)
        for s in range(4):
            base = pl.multiple_of(i * rows, rows) + s * SLAB
            mo[i, s] = gsec[pl.ds(base, SLAB), :][:part].astype(BF16)

    def take_upstream(i):
        for q in peers:
            gather_from(out_grad, uin, us_s, us_r, i, q).wait_recv()
        gather_own(out_grad, uin, us_r, i).wait()
        at = image_rows(i)
        up = widen_rows(uin, i)
        up = jnp.where(me * ni + i < valid[0], up, 0.0)
        ups[at, :] = up.astype(BF16)
        ups_t[:, at] = up.T.astype(BF16)
        vecs[4:5, :] += jnp.sum(up, axis=0, keepdims=True)

    late = min(3, ni)

    def arrive(i):
        @pl.when(i < ni)
        def _():
            forward(i)

        @pl.when(i >= late)
        def _():
            take_upstream(i - late)

    def arrive_step(i, carry):
        arrive(i)
        return carry

    lax.fori_loop(0, ni + late, arrive_step, 0)

    def send_mixed(i):
        for q in peers:
            return_copy(mo, mixed_out, ms_s, ms_r, i, q).start()
        return_own(mo, mixed_out, ms_s, i).start()

    gsec[...] = jnp.zeros_like(gsec)

    def chunk_compute(b):
        cs = pl.ds(pl.multiple_of(b * FC, FC), FC)
        total = jnp.zeros((1, FC), F32)
        for i in range(ni):
            at = slice(i * rows, (i + 1) * rows)
            inner = dot(sec[at, :], w1[:, cs]) + chan_inbias[:, cs]
            grad = dot_nt(ups[at, :], w2[cs, :])
            activ, slope = gelu_and_slope(inner)
            act_s[at, :] = activ.astype(BF16)
            gi = grad * slope
            gi_s[at, :] = gi.astype(BF16)
            total += jnp.sum(gi, axis=0, keepdims=True)
        d_b1[:, cs] = total
        g_out = dot(ups_t[...], act_s[...]).astype(BF16)
        g_in = dot(sec_t[...], gi_s[...]).astype(BF16)
        for n in range(1):
            c = b * (1) + n
            blk[c, 0] = g_in[:, n * FC : (n + 1) * FC]
            blk[c, 1] = g_out[:, n * FC : (n + 1) * FC]
        gsec[...] += dot_nt(gi_s[...], w1[:, cs])

    def image_backward(i):
        for q in peers:
            return_copy(mo, mixed_out, ms_s, ms_r, i, q).wait_send()
        return_own(mo, mixed_out, ms_s, i).wait()
        at = image_rows(i)
        x = widen_rows(xin, i)
        xh, r = normalise(x + mixed_keep[at, :].astype(F32))
        gs = gsec[at, :]
        vecs[2:3, :] += jnp.sum(gs * xh, axis=0, keepdims=True)
        vecs[3:4, :] += jnp.sum(gs, axis=0, keepdims=True)
        q = gs * gain_two[...]
        gm = ups[at, :].astype(F32) + r * (
            q - jnp.mean(q, axis=-1, keepdims=True) - xh * jnp.mean(q * xh, axis=-1, keepdims=True)
        )
        gmb = gm.astype(BF16)
        xh, r = normalise(x)
        normed = (xh * gain_one[...] + shift_one[...]).astype(BF16)
        hid, slope = gelu_and_slope(dot(tin_t[...], normed) + tok_inbias[...])
        gw = (dot(tout[...], gmb) * slope).astype(BF16)
        d_tout[...] += dot_nt(gmb, hid.astype(BF16))
        d_tin[...] += dot_nt(normed, gw)
        ones = jnp.ones((8, width), BF16)
        d_tb[:, :ds] += dot_nt(ones, gw)
        d_tb[:, ds : ds + rows] += dot_nt(ones, gmb)
        gn = dot(tin[...], gw).astype(BF16).astype(F32)
        vecs[0:1, :] += jnp.sum(gn * xh, axis=0, keepdims=True)
        vecs[1:2, :] += jnp.sum(gn, axis=0, keepdims=True)
        q = gn * gain_one[...]
        pg = gm + r * (
            q - jnp.mean(q, axis=-1, keepdims=True) - xh * jnp.mean(q * xh, axis=-1, keepdims=True)
        )
        for s in range(4):
            mo[i, s] = pg[s * SLAB : s * SLAB + part].astype(BF16)
        for p in peers:
            return_copy(mo, patch_grad, ps_s, ps_r, i, p).start()
        return_own(mo, patch_grad, ps_s, i).start()

    def pack_small():
        at = 0
        for v, n in (
            [(vecs[k : k + 1, :], width) for k in range(5)]
            + [(d_tb[0:1, :], ds + rows)]
            + [(d_b1[...], dc)]
        ):
            for j in range(n // 128):
                r = spare_row(at, part)
                d_tin[r : r + 1, :128] = v[:, j * 128 : (j + 1) * 128]
                at += 1
        for j in range(ds // 128):
            cols = slice(j * 128, (j + 1) * 128)
            blk[nc, 0, j * rows : (j + 1) * rows, :128] = d_tin[:, cols].astype(BF16)
            blk[nc, 1, j * rows : (j + 1) * rows, :128] = d_tout[:, cols].astype(BF16)
        blk[nc, :, :, 128:] = jnp.zeros((2, width, FC - 128), BF16)

    def parts(k, c, lanes):
        def region(m, start, size):
            return blk.at[c, m, pl.ds(pl.multiple_of(start, 16), size), pl.ds(0, lanes)]

        def transfer(slot, src, dst, dev):
            return pltpu.make_async_remote_copy(
                src_ref=src,
                dst_ref=dst,
                send_sem=as_s.at[slot, c],
                recv_sem=as_r.at[slot, c],
                device_id=dev,
                device_id_type=MESH,
            )

        if k == 0:
            land = r0.at[lax.rem(c, 4), :, pl.ds(0, lanes)]
            copy = transfer(0, region(1 - core, 0, width), land, dev_sib)
            return [(0, copy, region(core, 0, width), land, dev_sib)]
        if k == 8:
            own = region(core, 0, width)
            return [(1, transfer(1, own, own, dev_sib), None, None, dev_sib)]
        out = []
        for n, (base, size, first, b1, final) in enumerate(
            (
                (0, SPLIT, dev_y, yb, dev_x),
                (SPLIT, width - SPLIT, dev_x, xb, dev_y),
            )
        ):
            half, quarter, eighth = size // 2, size // 4, size // 8
            o1 = base + b1 * half
            n1 = base + (1 - b1) * half
            o2 = o1 + zab * quarter
            n2 = o1 + (1 - zab) * quarter
            o3 = o2 + zbb * eighth
            n3 = o2 + (1 - zbb) * eighth
            dev = (first, dev_za, dev_zb, final, dev_zb, dev_za, first)[k - 1]
            slot = 2 * k + n
            if k < 5:
                start, count = ((n1, half), (n2, quarter), (n3, eighth), (o3, eighth))[k - 1]
                keep = ((o1, half), (o2, quarter), (o3, eighth), (o3, eighth))[k - 1]
                offset = (0, SPLIT // 2 // (1, 2, 4, 4)[k - 1])[n]
                land = (r1, r2, r3, r4)[k - 1].at[c, pl.ds(offset, count), pl.ds(0, lanes)]
                copy = transfer(slot, region(core, start, count), land, dev)
                out.append((slot, copy, region(core, *keep), land, dev))
            else:
                mine = region(core, *((o3, eighth), (o2, quarter), (o1, half))[k - 5])
                out.append((slot, transfer(slot, mine, mine, dev), None, None, dev))
        return out

    def export(c):
        return pltpu.make_async_copy(blk.at[c], sums.at[c], osem.at[c])

    enter = nc + EXTRA

    def done(n):
        rest = jnp.maximum(n - LEAD, 0) * (nc + ni - LEAD) // (enter + 1 - LEAD)
        return jnp.minimum(n, LEAD) + rest

    def proceed(k, c, lanes):
        following = parts(k + 1, c, lanes) if k < 8 else []
        done = parts(k, c, lanes)
        for n, (slot, copy, kept, land, dev) in enumerate(done):
            copy.wait()
            if k < 4:
                pl.semaphore_signal(free.at[slot, c], inc=1, device_id=dev, device_id_type=MESH)
            if kept is not None:
                kept[...] = (kept[...].astype(F32) + land[...].astype(F32)).astype(BF16)
            if len(following) == len(done):
                begin(k + 1, c, following[n])
        if len(following) != len(done):
            for part_ in following:
                begin(k + 1, c, part_)
        if k == 8:
            export(c).start()

    def begin(k, c, part_):
        slot, copy = part_[:2]
        if k >= 5:
            back = 0 if k == 8 else 2 * (8 - k) + slot % 2
            pl.semaphore_wait(free.at[back, c], 1)
        copy.start()

    def advance(k, u):
        e = u - WAIT[k]

        @pl.when(jnp.logical_and(e >= 0, e < nc))
        def _():
            proceed(k, e, FC)

        @pl.when(e == enter)
        def _():
            proceed(k, nc, FC // 2)

    def step(u, carry):
        for k in reversed(range(9)):
            advance(k, u)

        @pl.when(u < ni)
        def _():
            send_mixed(u)

        @pl.when(u <= enter)
        def _():
            def quantum(w, carry):
                @pl.when(w < nc)
                def _():
                    chunk_compute(w)

                @pl.when(w >= nc)
                def _():
                    image_backward(w - nc)

                return carry

            lax.fori_loop(done(u), done(u + 1), quantum, 0)

        @pl.when(u < nc)
        def _():
            begin(0, u, parts(0, u, FC)[0])

        @pl.when(u == enter)
        def _():
            pack_small()
            begin(0, nc, parts(0, nc, FC // 2)[0])

        return carry

    lax.fori_loop(0, enter + 1 + WAIT[-1], step, 0)

    def finish(i):
        for q in peers:
            gather_copy(patches, xin, xs_s, xs_r, i, q).wait_send()
            gather_copy(out_grad, uin, us_s, us_r, i, q).wait_send()
            return_from(mo, mixed_out, ms_s, ms_r, i, q).wait_recv()
            return_copy(mo, patch_grad, ps_s, ps_r, i, q).wait_send()
            return_from(mo, patch_grad, ps_s, ps_r, i, q).wait_recv()
        return_own(mo, patch_grad, ps_s, i).wait()

    each_image(finish)

    def exported(c, carry):
        export(c).wait()
        return carry

    lax.fori_loop(0, nc + 1, exported, 0)


def spread_kernel(
    dims,
    block,
    small,
    mixed_from,
    patch_from,
    chan_in,
    chan_out,
    tok_in,
    tok_out_t,
    gain_one,
    shift_one,
    tok_inbias,
    tok_outbias,
    gain_two,
    shift_two,
    chan_inbias,
    chan_outbias,
    mixed_to,
    patch_to,
    hold,
    sem,
):
    ni, part, width, ds, dc = dims
    rows = 4 * SLAB
    loads = (
        pltpu.make_async_copy(mixed_from, hold.at[0], sem.at[0]),
        pltpu.make_async_copy(patch_from, hold.at[1], sem.at[1]),
    )
    stores = (
        pltpu.make_async_copy(hold.at[0], mixed_to, sem.at[2]),
        pltpu.make_async_copy(hold.at[1], patch_to, sem.at[3]),
    )

    @pl.when(pl.program_id(0) == 0)
    def _():
        for copy in loads:
            copy.start()

    @pl.when(pl.program_id(0) == pl.num_programs(0) // 2)
    def _():
        for load, store in zip(loads, stores):
            load.wait()
            store.start()

    @pl.when(pl.program_id(0) == pl.num_programs(0) - 1)
    def _():
        for store in stores:
            store.wait()

    for n in range(WIDE):
        chan_in[:, n * FC : (n + 1) * FC] = block[n, 0].astype(F32)
        chan_out[n * FC : (n + 1) * FC, :] = block[n, 1].astype(F32).T

    @pl.when(pl.program_id(0) == 0)
    def _():
        for m, ref in ((0, tok_in), (1, tok_out_t)):
            for j in range(ds // 128):
                v = small[0, m, j * rows : (j + 1) * rows, :128].astype(F32)
                for s in range(4):
                    ref[s * part : (s + 1) * part, j * 128 : (j + 1) * 128] = v[
                        s * SLAB : s * SLAB + part
                    ]
        v = small[0, 0, :rows, :128].astype(F32)
        at = 0
        for ref, n in (
            (gain_one, width),
            (shift_one, width),
            (gain_two, width),
            (shift_two, width),
            (chan_outbias, width),
            (tok_inbias, ds),
            (tok_outbias, rows),
            (chan_inbias, dc),
        ):
            picked = [spare_row(at + j, part) for j in range(n // 128)]
            flat = jnp.concatenate([v[r : r + 1] for r in picked], axis=1)
            at += n // 128
            if ref is tok_outbias:
                flat = jnp.concatenate(
                    [flat[:, s * SLAB : s * SLAB + part] for s in range(4)], axis=1
                )
            ref[...] = flat.reshape(ref.shape)


def shards(
    mesh_shape,
    patches,
    valid_counts,
    gain_one,
    shift_one,
    tok_in,
    tok_inbias,
    tok_out,
    tok_outbias,
    gain_two,
    shift_two,
    chan_in,
    chan_inbias,
    chan_out,
    chan_outbias,
    out_grad,
):
    images, part, width = patches.shape
    s_all, ds = tok_in.shape
    dc = chan_in.shape[1]
    ni = images // 4
    rows = 4 * SLAB
    total = ni * rows
    nc = dc // FC
    dims = (ni, part, width, ds, dc)
    anywhere = pl.BlockSpec(memory_space=pl.ANY)
    vmem = pl.BlockSpec(memory_space=pltpu.VMEM)
    dma = pltpu.SemaphoreType.DMA
    mixed_here, patch_here, sums = pl.pallas_call(
        functools.partial(layer_kernel, dims),
        name="layer",
        out_shape=(
            jax.ShapeDtypeStruct(patches.shape, BF16),
            jax.ShapeDtypeStruct(patches.shape, BF16),
            jax.ShapeDtypeStruct((nc + 1, 2, width, FC), BF16),
        ),
        in_specs=[anywhere] * 2
        + [pl.BlockSpec(memory_space=pltpu.SMEM)]
        + [vmem] * 2
        + [anywhere] * 2
        + [vmem] * 8,
        out_specs=(anywhere,) * 3,
        scratch_shapes=[
            pltpu.VMEM((width, dc), BF16),
            pltpu.VMEM((dc, width), BF16),
            pltpu.VMEM((ni, 4, part, width), BF16),
            pltpu.VMEM((ni, 4, part, width), BF16),
            pltpu.VMEM((ni, 4, part, width), BF16),
            pltpu.VMEM((rows, width), F32),
            pltpu.VMEM((rows, ds), BF16),
            pltpu.VMEM((ds, rows), BF16),
            pltpu.VMEM((ds, rows), BF16),
            pltpu.VMEM((rows, ds), BF16),
            pltpu.VMEM((total, width), BF16),
            pltpu.VMEM((total, width), BF16),
            pltpu.VMEM((width, total), BF16),
            pltpu.VMEM((total, width), BF16),
            pltpu.VMEM((width, total), BF16),
            pltpu.VMEM((total, width), F32),
            pltpu.VMEM((total, FC), BF16),
            pltpu.VMEM((total, FC), BF16),
            pltpu.VMEM((rows, ds), F32),
            pltpu.VMEM((rows, ds), F32),
            pltpu.VMEM((8, width), F32),
            pltpu.VMEM((1, dc), F32),
            pltpu.VMEM((8, ds + rows), F32),
            pltpu.VMEM((1, width), F32),
            pltpu.VMEM((1, width), F32),
            pltpu.VMEM((1, width), F32),
            pltpu.VMEM((1, width), F32),
            pltpu.VMEM((1, width), F32),
            pltpu.VMEM((ds, 1), F32),
            pltpu.VMEM((rows, 1), F32),
            pltpu.VMEM((nc + 1, 2, width, FC), BF16),
            pltpu.VMEM((4, width, FC), BF16),
            pltpu.VMEM((nc + 1, width // 2, FC), BF16),
            pltpu.VMEM((nc + 1, width // 4, FC), BF16),
            pltpu.VMEM((nc + 1, width // 8, FC), BF16),
            pltpu.VMEM((nc + 1, width // 8, FC), BF16),
            dma((2,)),
            dma((nc + 1,)),
        ]
        + [dma((ni, 4))] * 8
        + [dma((16, nc + 1))] * 2
        + [pltpu.SemaphoreType.REGULAR((8, nc + 1))],
        compiler_params=pltpu.CompilerParams(
            collective_id=0, has_side_effects=True, vmem_limit_bytes=63 << 20
        ),
        cost_estimate=pl.CostEstimate(
            flops=14 * total * width * dc,
            bytes_accessed=40 << 20,
            transcendentals=total * dc,
        ),
    )(
        patches,
        out_grad,
        valid_counts,
        tok_in,
        tok_out.T,
        chan_in,
        chan_out,
        gain_one,
        shift_one,
        gain_two,
        shift_two,
        tok_inbias,
        tok_outbias,
        chan_inbias.reshape(1, dc),
        chan_outbias,
    )
    vec = lambda n: (jax.ShapeDtypeStruct((n,), F32), pl.BlockSpec((n,), lambda c: (0,)))
    vectors = [vec(n) for n in (width, width, ds, s_all, width, width, dc, width)]
    out = pl.pallas_call(
        functools.partial(spread_kernel, dims),
        name="spread",
        grid=(nc // WIDE,),
        out_shape=(
            jax.ShapeDtypeStruct((width, dc), F32),
            jax.ShapeDtypeStruct((dc, width), F32),
            jax.ShapeDtypeStruct((s_all, ds), F32),
            jax.ShapeDtypeStruct((s_all, ds), F32),
        )
        + tuple(v[0] for v in vectors)
        + (
            jax.ShapeDtypeStruct(patches.shape, BF16),
            jax.ShapeDtypeStruct(patches.shape, BF16),
        ),
        in_specs=[
            pl.BlockSpec((WIDE, 2, width, FC), lambda c: (c, 0, 0, 0)),
            pl.BlockSpec((1, 2, width, FC), lambda c: (nc, 0, 0, 0)),
            anywhere,
            anywhere,
        ],
        out_specs=(
            pl.BlockSpec((width, WIDE * FC), lambda c: (0, c)),
            pl.BlockSpec((WIDE * FC, width), lambda c: (c, 0)),
            pl.BlockSpec((s_all, ds), lambda c: (0, 0)),
            pl.BlockSpec((s_all, ds), lambda c: (0, 0)),
        )
        + tuple(v[1] for v in vectors)
        + (anywhere, anywhere),
        scratch_shapes=[pltpu.VMEM((2,) + patches.shape, BF16), dma((4,))],
        compiler_params=pltpu.CompilerParams(vmem_limit_bytes=63 << 20),
    )(sums, sums, mixed_here, patch_here)
    g_chan_in, g_chan_out, g_tok_in, g_tok_out_t = out[:4]
    g_one, s_one, b_tin, b_tout, g_two, s_two, b_cin, b_cout, mixed_out, patch_grad = out[4:]
    grads = (
        g_one,
        s_one,
        g_tok_in,
        b_tin,
        g_tok_out_t.T,
        b_tout,
        g_two,
        s_two,
        g_chan_in,
        b_cin,
        g_chan_out,
        b_cout,
    )
    if mesh_shape["dp"] > GROUP:
        count = mesh_shape["dp"] // GROUP
        groups = [[g * GROUP + j for g in range(count)] for j in range(GROUP)]
        grads = lax.psum(grads, "dp", axis_index_groups=groups)
    return (mixed_out, patch_grad) + grads


def solution(mesh):
    whole, split = P(), P("dp", "mix", None)
    return jax.shard_map(
        functools.partial(shards, dict(mesh.shape)),
        mesh=mesh,
        in_specs=(split, P("dp")) + (whole,) * 12 + (split,),
        out_specs=(split, split) + (whole,) * 12,
        check_vma=False,
    )
```

```python
import functools

import jax
import jax.numpy as jnp
from jax import lax
from jax.experimental import pallas as pl
from jax.experimental.pallas import tpu as pltpu
from jax.sharding import PartitionSpec as P

EPS = 1e-06
SQ = 0.7978845608028654
CU = 0.044715
GROUP = 8
WIDE = 2
LEAD = 8
EXTRA = 4
WAIT = (2, 4, 6, 8, 10, 12, 14, 17, 19)
SLAB = 64
FC = 256
SPLIT = 512
NT = (((1,), (1,)), ((), ()))
F32 = jnp.float32
BF16 = jnp.bfloat16
MESH = pl.DeviceIdType.MESH


def gelu_and_slope(v):
    v2 = v * v
    p = 0.5 + 0.5 * jnp.tanh(v * (SQ + (SQ * CU) * v2))
    g = v * p
    return g, p + g * (1.0 - p) * (2.0 * SQ + (6.0 * SQ * CU) * v2)


def gelu(v):
    return v * (0.5 + 0.5 * jnp.tanh(v * (SQ + (SQ * CU) * (v * v))))


def normalise(v):
    c = v - jnp.mean(v, axis=-1, keepdims=True)
    r = lax.rsqrt(jnp.mean(c * c, axis=-1, keepdims=True) + EPS)
    return c * r, r


def dot(a, b):
    return jnp.dot(a, b, preferred_element_type=F32)


def dot_nt(a, b):
    return lax.dot_general(a, b, NT, preferred_element_type=F32)


def spare_row(n, part):
    spare = SLAB - part
    return n // spare * SLAB + part + n % spare


def flip(index, bit, step):
    return index + step - 2 * step * bit


def layer_kernel(
    dims,
    patches,
    out_grad,
    valid,
    tok_in,
    tok_out_t,
    chan_in,
    chan_out,
    gain_one_flat,
    shift_one_flat,
    gain_two_flat,
    shift_two_flat,
    tok_inbias_flat,
    tok_outbias_flat,
    chan_inbias,
    chan_outbias_flat,
    mixed_out,
    patch_grad,
    sums,
    w1,
    w2,
    xin,
    uin,
    mo,
    rows32,
    tin,
    tin_t,
    tout,
    tout_t,
    mixed_keep,
    sec,
    sec_t,
    ups,
    ups_t,
    gsec,
    gi_s,
    act_s,
    d_tin,
    d_tout,
    vecs,
    d_b1,
    d_tb,
    gain_one,
    shift_one,
    gain_two,
    shift_two,
    chan_outbias,
    tok_inbias,
    tok_outbias,
    blk,
    r0,
    r1,
    r2,
    r3,
    r4,
    wsem,
    osem,
    xs_s,
    xs_r,
    us_s,
    us_r,
    ms_s,
    ms_r,
    ps_s,
    ps_r,
    as_s,
    as_r,
    free,
):
    ni, part, width, ds, dc = dims
    nc = dc // FC
    rows = 4 * SLAB
    me = lax.axis_index("mix")
    dp = lax.axis_index("dp")
    core = lax.rem(me, 2)
    xb = me // 2
    yb = lax.rem(dp, 2)
    zab = lax.rem(dp // 2, 2)
    zbb = lax.rem(dp // 4, 2)
    sib = flip(me, core, 1)
    xp = flip(me, xb, 2)
    diag = 3 - me
    peers = (xp, diag, sib)
    dev_sib = (dp, sib)
    dev_x = (dp, xp)
    dev_y = (flip(dp, yb, 1), me)
    dev_za = (flip(dp, zab, 2), me)
    dev_zb = (flip(dp, zbb, 4), me)

    wcopy1 = pltpu.make_async_copy(chan_in, w1, wsem.at[0])
    wcopy2 = pltpu.make_async_copy(chan_out, w2, wsem.at[1])
    wcopy1.start()
    wcopy2.start()

    barrier = pltpu.get_barrier_semaphore()
    for dev in ((dp, xp), (dp, diag), dev_sib, dev_y, dev_za, dev_zb):
        pl.semaphore_signal(barrier, inc=1, device_id=dev, device_id_type=MESH)
    pl.semaphore_wait(barrier, 6)

    def gather_copy(src, dst, ssem, rsem, i, q):
        return pltpu.make_async_remote_copy(
            src_ref=src.at[q * ni + i],
            dst_ref=dst.at[i, me],
            send_sem=ssem.at[i, q],
            recv_sem=rsem.at[i, me],
            device_id=(dp, q),
            device_id_type=MESH,
        )

    def gather_from(src, dst, ssem, rsem, i, q):
        return pltpu.make_async_remote_copy(
            src_ref=src.at[q * ni + i],
            dst_ref=dst.at[i, q],
            send_sem=ssem.at[i, q],
            recv_sem=rsem.at[i, q],
            device_id=(dp, q),
            device_id_type=MESH,
        )

    def gather_own(src, dst, rsem, i):
        return pltpu.make_async_copy(src.at[me * ni + i], dst.at[i, me], rsem.at[i, me])

    def return_copy(src, dst, ssem, rsem, i, q):
        return pltpu.make_async_remote_copy(
            src_ref=src.at[i, q],
            dst_ref=dst.at[me * ni + i],
            send_sem=ssem.at[i, q],
            recv_sem=rsem.at[i, me],
            device_id=(dp, q),
            device_id_type=MESH,
        )

    def return_from(src, dst, ssem, rsem, i, q):
        return pltpu.make_async_remote_copy(
            src_ref=src.at[i, q],
            dst_ref=dst.at[q * ni + i],
            send_sem=ssem.at[i, q],
            recv_sem=rsem.at[i, q],
            device_id=(dp, q),
            device_id_type=MESH,
        )

    def return_own(src, dst, ssem, i):
        return pltpu.make_async_copy(src.at[i, me], dst.at[me * ni + i], ssem.at[i, me])

    def each_image(fn):
        def body(i, carry):
            fn(i)
            return carry

        lax.fori_loop(0, ni, body, 0)

    def send_patches(i):
        for q in peers:
            gather_copy(patches, xin, xs_s, xs_r, i, q).start()
        gather_own(patches, xin, xs_r, i).start()

    each_image(send_patches)

    rows32[...] = jnp.zeros_like(rows32)
    for w_in, w_row, w_col in ((tok_in, tin, tin_t), (tok_out_t, tout_t, tout)):
        wide = w_in[...].astype(F32)
        rows32[:, :ds] = jnp.zeros((rows, ds), F32)
        for s in range(4):
            rows32[s * SLAB : s * SLAB + part, :ds] = wide[s * part : (s + 1) * part]
        full = rows32[:, :ds]
        w_row[...] = full.astype(BF16)
        w_col[...] = full.T.astype(BF16)
    for flat, row in (
        (gain_one_flat, gain_one),
        (shift_one_flat, shift_one),
        (gain_two_flat, gain_two),
        (shift_two_flat, shift_two),
        (chan_outbias_flat, chan_outbias),
    ):
        row[...] = flat[...].reshape(1, width)
    tok_inbias[...] = jnp.broadcast_to(tok_inbias_flat[...].reshape(1, ds), (8, ds)).T[:, :1]
    rows32[...] = jnp.zeros_like(rows32)
    rows32[:1, : 4 * part] = tok_outbias_flat[...].reshape(1, 4 * part)
    column = rows32[:8, :rows].T
    rows32[...] = jnp.zeros_like(rows32)
    for s in range(4):
        rows32[s * SLAB : s * SLAB + part, :8] = column[s * part : (s + 1) * part]
    tok_outbias[...] = rows32[:, :1]
    rows32[...] = jnp.zeros_like(rows32)
    d_tin[...] = jnp.zeros_like(d_tin)
    d_tout[...] = jnp.zeros_like(d_tout)
    vecs[...] = jnp.zeros_like(vecs)
    d_tb[...] = jnp.zeros_like(d_tb)

    def widen_rows(ref, i):
        for s in range(4):
            rows32[s * SLAB : s * SLAB + part, :] = ref[i, s].astype(F32)
        return rows32[...]

    def image_rows(i):
        return pl.ds(pl.multiple_of(i * rows, rows), rows)

    wcopy1.wait()
    wcopy2.wait()

    def forward(i):
        for q in peers:
            gather_from(patches, xin, xs_s, xs_r, i, q).wait_recv()
        gather_own(patches, xin, xs_r, i).wait()
        for q in peers:
            gather_copy(out_grad, uin, us_s, us_r, i, q).start()
        gather_own(out_grad, uin, us_r, i).start()
        at = image_rows(i)
        x = widen_rows(xin, i)
        xh, _ = normalise(x)
        normed = (xh * gain_one[...] + shift_one[...]).astype(BF16)
        hidden = gelu(dot(tin_t[...], normed) + tok_inbias[...]).astype(BF16)
        mixed = (dot(tout_t[...], hidden) + tok_outbias[...]).astype(BF16)
        mixed_keep[at, :] = mixed
        middle = x + mixed.astype(F32)
        xh, _ = normalise(middle)
        second = xh * gain_two[...] + shift_two[...]
        sec[at, :] = second.astype(BF16)
        sec_t[:, at] = second.T.astype(BF16)
        gsec[at, :] = middle + chan_outbias[...]

        def hidden_block(c, carry):
            cs = pl.ds(pl.multiple_of(c * 768, 768), 768)
            activ = gelu(dot(sec[at, :], w1[:, cs]) + chan_inbias[:, cs]).astype(BF16)
            gsec[at, :] += dot(activ, w2[cs, :])
            return carry

        lax.fori_loop(0, dc // 768, hidden_block, 0, unroll=True)
        for s in range(4):
            base = pl.multiple_of(i * rows, rows) + s * SLAB
            mo[i, s] = gsec[pl.ds(base, SLAB), :][:part].astype(BF16)

    def take_upstream(i):
        for q in peers:
            gather_from(out_grad, uin, us_s, us_r, i, q).wait_recv()
        gather_own(out_grad, uin, us_r, i).wait()
        at = image_rows(i)
        up = widen_rows(uin, i)
        up = jnp.where(me * ni + i < valid[0], up, 0.0)
        ups[at, :] = up.astype(BF16)
        ups_t[:, at] = up.T.astype(BF16)
        vecs[4:5, :] += jnp.sum(up, axis=0, keepdims=True)

    late = min(3, ni)

    def arrive(i):
        @pl.when(i < ni)
        def _():
            forward(i)

        @pl.when(i >= late)
        def _():
            take_upstream(i - late)

    def arrive_step(i, carry):
        arrive(i)
        return carry

    lax.fori_loop(0, ni + late, arrive_step, 0)

    def send_mixed(i):
        for q in peers:
            return_copy(mo, mixed_out, ms_s, ms_r, i, q).start()
        return_own(mo, mixed_out, ms_s, i).start()

    gsec[...] = jnp.zeros_like(gsec)

    def chunk_compute(b):
        cs = pl.ds(pl.multiple_of(b * FC, FC), FC)
        total = jnp.zeros((1, FC), F32)
        for i in range(ni):
            at = slice(i * rows, (i + 1) * rows)
            inner = dot(sec[at, :], w1[:, cs]) + chan_inbias[:, cs]
            grad = dot_nt(ups[at, :], w2[cs, :])
            activ, slope = gelu_and_slope(inner)
            act_s[at, :] = activ.astype(BF16)
            gi = grad * slope
            gi_s[at, :] = gi.astype(BF16)
            total += jnp.sum(gi, axis=0, keepdims=True)
        d_b1[:, cs] = total
        g_out = dot(ups_t[...], act_s[...]).astype(BF16)
        g_in = dot(sec_t[...], gi_s[...]).astype(BF16)
        for n in range(1):
            c = b * (1) + n
            blk[c, 0] = g_in[:, n * FC : (n + 1) * FC]
            blk[c, 1] = g_out[:, n * FC : (n + 1) * FC]
        gsec[...] += dot_nt(gi_s[...], w1[:, cs])

    def image_backward(i):
        for q in peers:
            return_copy(mo, mixed_out, ms_s, ms_r, i, q).wait_send()
        return_own(mo, mixed_out, ms_s, i).wait()
        at = image_rows(i)
        x = widen_rows(xin, i)
        xh, r = normalise(x + mixed_keep[at, :].astype(F32))
        gs = gsec[at, :]
        vecs[2:3, :] += jnp.sum(gs * xh, axis=0, keepdims=True)
        vecs[3:4, :] += jnp.sum(gs, axis=0, keepdims=True)
        q = gs * gain_two[...]
        gm = ups[at, :].astype(F32) + r * (
            q - jnp.mean(q, axis=-1, keepdims=True) - xh * jnp.mean(q * xh, axis=-1, keepdims=True)
        )
        gmb = gm.astype(BF16)
        xh, r = normalise(x)
        normed = (xh * gain_one[...] + shift_one[...]).astype(BF16)
        hid, slope = gelu_and_slope(dot(tin_t[...], normed) + tok_inbias[...])
        gw = (dot(tout[...], gmb) * slope).astype(BF16)
        d_tout[...] += dot_nt(gmb, hid.astype(BF16))
        d_tin[...] += dot_nt(normed, gw)
        ones = jnp.ones((8, width), BF16)
        d_tb[:, :ds] += dot_nt(ones, gw)
        d_tb[:, ds : ds + rows] += dot_nt(ones, gmb)
        gn = dot(tin[...], gw).astype(BF16).astype(F32)
        vecs[0:1, :] += jnp.sum(gn * xh, axis=0, keepdims=True)
        vecs[1:2, :] += jnp.sum(gn, axis=0, keepdims=True)
        q = gn * gain_one[...]
        pg = gm + r * (
            q - jnp.mean(q, axis=-1, keepdims=True) - xh * jnp.mean(q * xh, axis=-1, keepdims=True)
        )
        for s in range(4):
            mo[i, s] = pg[s * SLAB : s * SLAB + part].astype(BF16)
        for p in peers:
            return_copy(mo, patch_grad, ps_s, ps_r, i, p).start()
        return_own(mo, patch_grad, ps_s, i).start()

    def pack_small():
        at = 0
        for v, n in (
            [(vecs[k : k + 1, :], width) for k in range(5)]
            + [(d_tb[0:1, :], ds + rows)]
            + [(d_b1[...], dc)]
        ):
            for j in range(n // 128):
                r = spare_row(at, part)
                d_tin[r : r + 1, :128] = v[:, j * 128 : (j + 1) * 128]
                at += 1
        for j in range(ds // 128):
            cols = slice(j * 128, (j + 1) * 128)
            blk[nc, 0, j * rows : (j + 1) * rows, :128] = d_tin[:, cols].astype(BF16)
            blk[nc, 1, j * rows : (j + 1) * rows, :128] = d_tout[:, cols].astype(BF16)
        blk[nc, :, :, 128:] = jnp.zeros((2, width, FC - 128), BF16)

    def parts(k, c, lanes):
        def region(m, start, size):
            return blk.at[c, m, pl.ds(pl.multiple_of(start, 16), size), pl.ds(0, lanes)]

        def transfer(slot, src, dst, dev):
            return pltpu.make_async_remote_copy(
                src_ref=src,
                dst_ref=dst,
                send_sem=as_s.at[slot, lax.rem(c, 4)],
                recv_sem=as_r.at[slot, c],
                device_id=dev,
                device_id_type=MESH,
            )

        if k == 0:
            land = r0.at[lax.rem(c, 4), :, pl.ds(0, lanes)]
            copy = transfer(0, region(1 - core, 0, width), land, dev_sib)
            return [(0, copy, region(core, 0, width), land, dev_sib)]
        if k == 8:
            own = region(core, 0, width)
            return [(1, transfer(1, own, own, dev_sib), None, None, dev_sib)]
        out = []
        for n, (base, size, first, b1, final) in enumerate(
            (
                (0, SPLIT, dev_y, yb, dev_x),
                (SPLIT, width - SPLIT, dev_x, xb, dev_y),
            )
        ):
            half, quarter, eighth = size // 2, size // 4, size // 8
            o1 = base + b1 * half
            n1 = base + (1 - b1) * half
            o2 = o1 + zab * quarter
            n2 = o1 + (1 - zab) * quarter
            o3 = o2 + zbb * eighth
            n3 = o2 + (1 - zbb) * eighth
            dev = (first, dev_za, dev_zb, final, dev_zb, dev_za, first)[k - 1]
            slot = 2 * k + n
            if k < 5:
                start, count = ((n1, half), (n2, quarter), (n3, eighth), (o3, eighth))[k - 1]
                keep = ((o1, half), (o2, quarter), (o3, eighth), (o3, eighth))[k - 1]
                offset = (0, SPLIT // 2 // (1, 2, 4, 4)[k - 1])[n]
                land = (r1, r2, r3, r4)[k - 1].at[c, pl.ds(offset, count), pl.ds(0, lanes)]
                copy = transfer(slot, region(core, start, count), land, dev)
                out.append((slot, copy, region(core, *keep), land, dev))
            else:
                mine = region(core, *((o3, eighth), (o2, quarter), (o1, half))[k - 5])
                out.append((slot, transfer(slot, mine, mine, dev), None, None, dev))
        return out

    def export(c):
        return pltpu.make_async_copy(blk.at[c], sums.at[c], osem.at[c])

    enter = nc + EXTRA

    def done(n):
        rest = jnp.maximum(n - LEAD, 0) * (nc + ni - LEAD) // (enter + 1 - LEAD)
        return jnp.minimum(n, LEAD) + rest

    def proceed(k, c, lanes):
        following = parts(k + 1, c, lanes) if k < 8 else []
        done = parts(k, c, lanes)
        for n, (slot, copy, kept, land, dev) in enumerate(done):
            copy.wait()
            if k < 4:
                pl.semaphore_signal(free.at[slot, c], inc=1, device_id=dev, device_id_type=MESH)
            if kept is not None:
                kept[...] = (kept[...].astype(F32) + land[...].astype(F32)).astype(BF16)
            if len(following) == len(done):
                begin(k + 1, c, following[n])
        if len(following) != len(done):
            for part_ in following:
                begin(k + 1, c, part_)
        if k == 8:
            export(c).start()

    def begin(k, c, part_):
        slot, copy = part_[:2]
        if k >= 5:
            back = 0 if k == 8 else 2 * (8 - k) + slot % 2
            pl.semaphore_wait(free.at[back, c], 1)
        copy.start()

    def advance(k, u):
        e = u - WAIT[k]

        @pl.when(jnp.logical_and(e >= 0, e < nc))
        def _():
            proceed(k, e, FC)

        @pl.when(e == enter)
        def _():
            proceed(k, nc, FC // 2)

    def step(u, carry):
        for k in reversed(range(9)):
            advance(k, u)

        @pl.when(u < ni)
        def _():
            send_mixed(u)

        @pl.when(u <= enter)
        def _():
            def quantum(w, carry):
                @pl.when(w < nc)
                def _():
                    chunk_compute(w)

                @pl.when(w >= nc)
                def _():
                    image_backward(w - nc)

                return carry

            lax.fori_loop(done(u), done(u + 1), quantum, 0)

        @pl.when(u < nc)
        def _():
            begin(0, u, parts(0, u, FC)[0])

        @pl.when(u == enter)
        def _():
            pack_small()
            begin(0, nc, parts(0, nc, FC // 2)[0])

        return carry

    lax.fori_loop(0, enter + 1 + WAIT[-1], step, 0)

    def finish(i):
        for q in peers:
            gather_copy(patches, xin, xs_s, xs_r, i, q).wait_send()
            gather_copy(out_grad, uin, us_s, us_r, i, q).wait_send()
            return_from(mo, mixed_out, ms_s, ms_r, i, q).wait_recv()
            return_copy(mo, patch_grad, ps_s, ps_r, i, q).wait_send()
            return_from(mo, patch_grad, ps_s, ps_r, i, q).wait_recv()
        return_own(mo, patch_grad, ps_s, i).wait()

    each_image(finish)

    def exported(c, carry):
        export(c).wait()
        return carry

    lax.fori_loop(0, nc + 1, exported, 0)


def spread_kernel(
    dims,
    block,
    small,
    mixed_from,
    patch_from,
    chan_in,
    chan_out,
    tok_in,
    tok_out_t,
    gain_one,
    shift_one,
    tok_inbias,
    tok_outbias,
    gain_two,
    shift_two,
    chan_inbias,
    chan_outbias,
    mixed_to,
    patch_to,
    hold,
    sem,
):
    ni, part, width, ds, dc = dims
    rows = 4 * SLAB
    loads = (
        pltpu.make_async_copy(mixed_from, hold.at[0], sem.at[0]),
        pltpu.make_async_copy(patch_from, hold.at[1], sem.at[1]),
    )
    stores = (
        pltpu.make_async_copy(hold.at[0], mixed_to, sem.at[2]),
        pltpu.make_async_copy(hold.at[1], patch_to, sem.at[3]),
    )

    @pl.when(pl.program_id(0) == 0)
    def _():
        for copy in loads:
            copy.start()

    @pl.when(pl.program_id(0) == pl.num_programs(0) // 2)
    def _():
        for load, store in zip(loads, stores):
            load.wait()
            store.start()

    @pl.when(pl.program_id(0) == pl.num_programs(0) - 1)
    def _():
        for store in stores:
            store.wait()

    for n in range(WIDE):
        chan_in[:, n * FC : (n + 1) * FC] = block[n, 0].astype(F32)
        chan_out[n * FC : (n + 1) * FC, :] = block[n, 1].astype(F32).T

    @pl.when(pl.program_id(0) == 0)
    def _():
        for m, ref in ((0, tok_in), (1, tok_out_t)):
            for j in range(ds // 128):
                v = small[0, m, j * rows : (j + 1) * rows, :128].astype(F32)
                for s in range(4):
                    ref[s * part : (s + 1) * part, j * 128 : (j + 1) * 128] = v[
                        s * SLAB : s * SLAB + part
                    ]
        v = small[0, 0, :rows, :128].astype(F32)
        at = 0
        for ref, n in (
            (gain_one, width),
            (shift_one, width),
            (gain_two, width),
            (shift_two, width),
            (chan_outbias, width),
            (tok_inbias, ds),
            (tok_outbias, rows),
            (chan_inbias, dc),
        ):
            picked = [spare_row(at + j, part) for j in range(n // 128)]
            flat = jnp.concatenate([v[r : r + 1] for r in picked], axis=1)
            at += n // 128
            if ref is tok_outbias:
                flat = jnp.concatenate(
                    [flat[:, s * SLAB : s * SLAB + part] for s in range(4)], axis=1
                )
            ref[...] = flat.reshape(ref.shape)


def shards(
    mesh_shape,
    patches,
    valid_counts,
    gain_one,
    shift_one,
    tok_in,
    tok_inbias,
    tok_out,
    tok_outbias,
    gain_two,
    shift_two,
    chan_in,
    chan_inbias,
    chan_out,
    chan_outbias,
    out_grad,
):
    images, part, width = patches.shape
    s_all, ds = tok_in.shape
    dc = chan_in.shape[1]
    ni = images // 4
    rows = 4 * SLAB
    total = ni * rows
    nc = dc // FC
    dims = (ni, part, width, ds, dc)
    anywhere = pl.BlockSpec(memory_space=pl.ANY)
    vmem = pl.BlockSpec(memory_space=pltpu.VMEM)
    dma = pltpu.SemaphoreType.DMA
    mixed_here, patch_here, sums = pl.pallas_call(
        functools.partial(layer_kernel, dims),
        name="layer",
        out_shape=(
            jax.ShapeDtypeStruct(patches.shape, BF16),
            jax.ShapeDtypeStruct(patches.shape, BF16),
            jax.ShapeDtypeStruct((nc + 1, 2, width, FC), BF16),
        ),
        in_specs=[anywhere] * 2
        + [pl.BlockSpec(memory_space=pltpu.SMEM)]
        + [vmem] * 2
        + [anywhere] * 2
        + [vmem] * 8,
        out_specs=(anywhere,) * 3,
        scratch_shapes=[
            pltpu.VMEM((width, dc), BF16),
            pltpu.VMEM((dc, width), BF16),
            pltpu.VMEM((ni, 4, part, width), BF16),
            pltpu.VMEM((ni, 4, part, width), BF16),
            pltpu.VMEM((ni, 4, part, width), BF16),
            pltpu.VMEM((rows, width), F32),
            pltpu.VMEM((rows, ds), BF16),
            pltpu.VMEM((ds, rows), BF16),
            pltpu.VMEM((ds, rows), BF16),
            pltpu.VMEM((rows, ds), BF16),
            pltpu.VMEM((total, width), BF16),
            pltpu.VMEM((total, width), BF16),
            pltpu.VMEM((width, total), BF16),
            pltpu.VMEM((total, width), BF16),
            pltpu.VMEM((width, total), BF16),
            pltpu.VMEM((total, width), F32),
            pltpu.VMEM((total, FC), BF16),
            pltpu.VMEM((total, FC), BF16),
            pltpu.VMEM((rows, ds), F32),
            pltpu.VMEM((rows, ds), F32),
            pltpu.VMEM((8, width), F32),
            pltpu.VMEM((1, dc), F32),
            pltpu.VMEM((8, ds + rows), F32),
            pltpu.VMEM((1, width), F32),
            pltpu.VMEM((1, width), F32),
            pltpu.VMEM((1, width), F32),
            pltpu.VMEM((1, width), F32),
            pltpu.VMEM((1, width), F32),
            pltpu.VMEM((ds, 1), F32),
            pltpu.VMEM((rows, 1), F32),
            pltpu.VMEM((nc + 1, 2, width, FC), BF16),
            pltpu.VMEM((4, width, FC), BF16),
            pltpu.VMEM((nc + 1, width // 2, FC), BF16),
            pltpu.VMEM((nc + 1, width // 4, FC), BF16),
            pltpu.VMEM((nc + 1, width // 8, FC), BF16),
            pltpu.VMEM((nc + 1, width // 8, FC), BF16),
            dma((2,)),
            dma((nc + 1,)),
        ]
        + [dma((ni, 4))] * 8
        + [dma((16, 4)), dma((16, nc + 1))]
        + [pltpu.SemaphoreType.REGULAR((8, nc + 1))],
        compiler_params=pltpu.CompilerParams(
            collective_id=0, has_side_effects=True, vmem_limit_bytes=63 << 20
        ),
        cost_estimate=pl.CostEstimate(
            flops=14 * total * width * dc,
            bytes_accessed=40 << 20,
            transcendentals=total * dc,
        ),
    )(
        patches,
        out_grad,
        valid_counts,
        tok_in,
        tok_out.T,
        chan_in,
        chan_out,
        gain_one,
        shift_one,
        gain_two,
        shift_two,
        tok_inbias,
        tok_outbias,
        chan_inbias.reshape(1, dc),
        chan_outbias,
    )
    vec = lambda n: (jax.ShapeDtypeStruct((n,), F32), pl.BlockSpec((n,), lambda c: (0,)))
    vectors = [vec(n) for n in (width, width, ds, s_all, width, width, dc, width)]
    out = pl.pallas_call(
        functools.partial(spread_kernel, dims),
        name="spread",
        grid=(nc // WIDE,),
        out_shape=(
            jax.ShapeDtypeStruct((width, dc), F32),
            jax.ShapeDtypeStruct((dc, width), F32),
            jax.ShapeDtypeStruct((s_all, ds), F32),
            jax.ShapeDtypeStruct((s_all, ds), F32),
        )
        + tuple(v[0] for v in vectors)
        + (
            jax.ShapeDtypeStruct(patches.shape, BF16),
            jax.ShapeDtypeStruct(patches.shape, BF16),
        ),
        in_specs=[
            pl.BlockSpec((WIDE, 2, width, FC), lambda c: (c, 0, 0, 0)),
            pl.BlockSpec((1, 2, width, FC), lambda c: (nc, 0, 0, 0)),
            anywhere,
            anywhere,
        ],
        out_specs=(
            pl.BlockSpec((width, WIDE * FC), lambda c: (0, c)),
            pl.BlockSpec((WIDE * FC, width), lambda c: (c, 0)),
            pl.BlockSpec((s_all, ds), lambda c: (0, 0)),
            pl.BlockSpec((s_all, ds), lambda c: (0, 0)),
        )
        + tuple(v[1] for v in vectors)
        + (anywhere, anywhere),
        scratch_shapes=[pltpu.VMEM((2,) + patches.shape, BF16), dma((4,))],
        compiler_params=pltpu.CompilerParams(vmem_limit_bytes=63 << 20),
    )(sums, sums, mixed_here, patch_here)
    g_chan_in, g_chan_out, g_tok_in, g_tok_out_t = out[:4]
    g_one, s_one, b_tin, b_tout, g_two, s_two, b_cin, b_cout, mixed_out, patch_grad = out[4:]
    grads = (
        g_one,
        s_one,
        g_tok_in,
        b_tin,
        g_tok_out_t.T,
        b_tout,
        g_two,
        s_two,
        g_chan_in,
        b_cin,
        g_chan_out,
        b_cout,
    )
    if mesh_shape["dp"] > GROUP:
        count = mesh_shape["dp"] // GROUP
        groups = [[g * GROUP + j for g in range(count)] for j in range(GROUP)]
        grads = lax.psum(grads, "dp", axis_index_groups=groups)
    return (mixed_out, patch_grad) + grads


def solution(mesh):
    whole, split = P(), P("dp", "mix", None)
    return jax.shard_map(
        functools.partial(shards, dict(mesh.shape)),
        mesh=mesh,
        in_specs=(split, P("dp")) + (whole,) * 12 + (split,),
        out_specs=(split, split) + (whole,) * 12,
        check_vma=False,
    )
```
